256 devices in a mesh: group: 8 (over x, core), ctx: 32 (over z, y).
Axes of the slice: x: 4, y: 4, z: 8, core: 2. Of those that a mesh axis runs over, the one named last changes fastest.
Arguments:
- series: bfloat16 [65536, 768], P(('group', 'ctx')), may hold values from -6 to 6
- recon_mask: int32 [65536], P(('group', 'ctx')), may hold values 0 or 1
- mask_token: bfloat16 [768], replicated, may hold values from -4 to 4
- packing_list: int32 [2048], P(('group', 'ctx')), may hold values from 0 to 7, as said below
- doc_ids: int32 [8, 8192], P('group', 'ctx'), may hold values from 0 to 3, never falling along the last dimension, each value on 1 to 5120 neighbouring positions
- norm_gain: bfloat16 [768], replicated, may hold values from 0.099609375 to 1.8984375
- w_query: bfloat16 [768, 768], replicated
- w_key: bfloat16 [768, 768], replicated
- w_value: bfloat16 [768, 768], replicated, may hold values from -0.21875 to 0.21875
- w_out: bfloat16 [768, 768], replicated, may hold values from -0.21875 to 0.21875
Outputs:
- encoded: bfloat16 [65536, 768], P(('group', 'ctx'))
The draws below stay inside these ranges and needn't reach their ends.
Inputs may be any that keep to these rules, and one draw needn't show every extreme that they name: `packing_list`: the 8 consecutive entries of each arrival block (one device of the arrival layout) name every packed group exactly once.
All inputs are finite; a program needn't handle non-finite values. No bound on the sum of `recon_mask` on one device may be relied on, other than what follows from the above.
Results may differ from the reference program's by a relative error of at most 0.005.
Values may be sent and summed in bfloat16 or wider, within the bound.
A program may use at most 128 MiB of HBM per device.

```python
import math
import jax
import jax.numpy as jnp
import numpy as np
from jax import lax

D = 768
HEADS = 12
HD = 64
DOCS = 4
BLK = 32
GROUP_TOK = 8192
DOC_MOST = 5120
TOKENS = 65536
N_GROUP = 8
N_CTX = 32


def draw_packing_list(key, part):
    device_keys = jax.random.split(key, N_GROUP * N_CTX)
    listed = jax.vmap(lambda single: jax.random.permutation(single, N_GROUP))(device_keys)
    return listed.reshape(-1).astype(jnp.int32)


def query_matrix(key):
    return jax.random.normal(jax.random.fold_in(key, 11), (D, D), jnp.float32) / math.sqrt(D)


def draw_w_query(key, part):
    return query_matrix(key).astype(jnp.bfloat16)


def draw_w_key(key, part):
    fresh = jax.random.normal(jax.random.fold_in(key, 12), (D, D), jnp.float32) / math.sqrt(D)
    return fresh.astype(jnp.bfloat16)


def plant(values, stream_key, low, high):
    place = [jax.random.randint(jax.random.fold_in(stream_key, axis), (), 0, length) for axis, length in enumerate(values.shape)]
    longest = values.shape.index(max(values.shape))
    beside = place[:longest] + [(place[longest] + 1) % values.shape[longest]] + place[longest + 1:]
    return values.at[tuple(place)].set(low).at[tuple(beside)].set(high)


def shard_levels(key, shape, cuts, smallest, top_value):
    def one(dim, blocks):
        heights = jax.random.uniform(jax.random.fold_in(jax.random.fold_in(key, 6), dim), (blocks,), jnp.float32, smallest / len(cuts), top_value / len(cuts))
        return jnp.repeat(jnp.exp(heights), shape[dim] // blocks).reshape((-1,) + (1,) * (len(shape) - dim - 1))

    level = one(*cuts[0])
    for cut in cuts[1:]:
        level = level * one(*cut)
    return level


def length_profile(number_of, total, reach, skew):
    loads = [(1 << 20) // math.isqrt(standing ** skew) + 1 for standing in range(2, number_of + 1)]
    rest, counts = total - reach - (number_of - 1), [1] * (number_of - 1)
    while rest > 0:
        movable = [i for i in range(number_of - 1) if counts[i] < reach]
        mass, left = sum([loads[i] for i in movable]), rest
        for i in movable:
            extra = min(reach - counts[i], max(1, left * loads[i] // mass), rest)
            counts[i] = counts[i] + extra
            rest = rest - extra
    return np.array([reach] + counts)


def uneven_parts(own_key, amount, total, most, slope):
    if amount == 2:
        one = jax.random.randint(own_key, (), max(1, total - most), min(most, total - 1) + 1)
        return jnp.stack([one, total - one])
    lengths = jnp.asarray(length_profile(amount, total, most, slope), jnp.int32)
    pairs = (amount - 1) // 2
    donor, taker = lengths[1:1 + 2 * pairs:2], lengths[2:2 + 2 * pairs:2]
    room = jnp.minimum(donor - 1, most - taker)
    shifted = jax.random.randint(jax.random.fold_in(own_key, 1), (pairs,), 0, 1 << 20) % (room + 1)
    lengths = lengths.at[1:1 + 2 * pairs:2].set(donor - shifted).at[2:2 + 2 * pairs:2].set(taker + shifted)
    return lengths[jax.random.permutation(jax.random.fold_in(own_key, 2), amount)]


def centred(stream_key, dims, spread, reach, cuts=(), kind=jnp.bfloat16):
    loudness = shard_levels(stream_key, dims, cuts, -0.22, 0.18) if cuts else 1.0
    drawn = jax.random.normal(stream_key, dims, jnp.float32) * spread * loudness
    return jnp.minimum(jnp.maximum(drawn, -reach), reach).astype(kind)


def setup_inputs(seed: int = 0) -> dict:
    key_list = jax.random.split(jax.random.key(seed), 11)
    return {
        "series": centred(key_list[0], (TOKENS, D), 1.0, 6.0, ((0, 256),)),
        "recon_mask": plant((jax.random.randint(key_list[1], (TOKENS,), 0, 20) < 3).astype(jnp.int32), jax.random.fold_in(key_list[1], 1), 0, 1),
        "mask_token": centred(key_list[2], (D,), 1.0, 4.0),
        "packing_list": draw_packing_list(jax.random.fold_in(key_list[10], 71), 0),
        "doc_ids": jax.vmap(lambda own: jnp.searchsorted(jnp.cumsum(uneven_parts(own, DOCS, GROUP_TOK, DOC_MOST, 0)), jnp.arange(GROUP_TOK), side="right"))(jax.random.split(key_list[4], N_GROUP)).reshape((N_GROUP, GROUP_TOK)).astype(jnp.int32),
        "norm_gain": jnp.clip(1.0 + 0.18 * jax.random.normal(key_list[5], (D,), jnp.float32), 0.099609375, 1.8984375).astype(jnp.bfloat16),
        "w_query": draw_w_query(jax.random.fold_in(key_list[10], 71), 0),
        "w_key": draw_w_key(jax.random.fold_in(key_list[10], 71), 0),
        "w_value": centred(key_list[8], (D, D), D ** -0.5, 0.21875),
        "w_out": centred(key_list[9], (D, D), D ** -0.5, 0.21875),
    }


NEGATIVE = -1e+30

def rms_normed(values, gain):
    widened = values.astype(jnp.float32)
    factor = lax.rsqrt(lax.optimization_barrier(jnp.mean(widened * widened, axis=-1, keepdims=True)) + 1e-06)
    return (widened * factor * gain.astype(jnp.float32)[None, :]).astype(jnp.bfloat16)

def attend_group(arguments, norm_gain, w_query, w_key, w_value, w_out):
    packed, documents = arguments
    group_rows = packed.shape[0]
    normed = rms_normed(packed, norm_gain)
    query = jnp.dot(normed, w_query, preferred_element_type=jnp.float32).astype(jnp.bfloat16)
    keyed = jnp.dot(normed, w_key, preferred_element_type=jnp.float32).astype(jnp.bfloat16)
    valued = jnp.dot(normed, w_value, preferred_element_type=jnp.float32).astype(jnp.bfloat16)
    head_key = keyed.reshape(group_rows, HEADS, HD).astype(jnp.float32)
    head_value = valued.reshape(group_rows, HEADS, HD).astype(jnp.float32)
    block_rows = math.gcd(group_rows, 512)
    block_count = group_rows // block_rows
    query_blocks = query.reshape(block_count, block_rows, HEADS, HD)
    doc_blocks = documents.reshape(block_count, block_rows)

    def one_block(block_args):
        query_block, doc_block = block_args
        scores = jnp.einsum('qhd,khd->hqk', query_block.astype(jnp.float32), head_key) * (1.0 / math.sqrt(HD))
        allowed = (doc_block[:, None] == documents[None, :])[None]
        scores = jnp.where(allowed, scores, NEGATIVE)
        rowmax = lax.optimization_barrier(jnp.max(scores, axis=-1, keepdims=True))
        expo = jnp.where(allowed, jnp.exp(scores - rowmax), 0.0)
        totals = lax.optimization_barrier(jnp.sum(expo, axis=-1))
        weights = lax.optimization_barrier(expo.astype(jnp.bfloat16)).astype(jnp.float32)
        summed = jnp.einsum('hqk,khd->hqd', weights, head_value) / totals[..., None]
        return summed.transpose(1, 0, 2).reshape(block_rows, D).astype(jnp.bfloat16)
    attended = lax.map(one_block, (query_blocks, doc_blocks)).reshape(group_rows, D)
    mixed = jnp.dot(attended, w_out, preferred_element_type=jnp.float32)
    return (packed.astype(jnp.float32) + mixed).astype(jnp.bfloat16)

def reference(series, recon_mask, mask_token, packing_list, doc_ids, norm_gain, w_query, w_key, w_value, w_out):
    masked = jnp.where(recon_mask[:, None] == 1, mask_token[None, :], series)
    pieces = masked.reshape(N_GROUP, N_CTX, N_GROUP, BLK, D)
    targets = packing_list.reshape(N_GROUP, N_CTX, N_GROUP).astype(jnp.int32)
    inverse = jnp.argsort(targets, axis=-1).astype(jnp.int32)
    chosen = jnp.take_along_axis(pieces, inverse[:, :, :, None, None], axis=2)
    packed = chosen.transpose(2, 1, 0, 3, 4).reshape(N_GROUP, GROUP_TOK, D)

    def per_group(group_args):
        return attend_group(group_args, norm_gain, w_query, w_key, w_value, w_out)
    out_packed = lax.map(per_group, (packed, doc_ids))
    by_slot = out_packed.reshape(N_GROUP, N_CTX, N_GROUP, BLK, D).transpose(2, 1, 0, 3, 4)
    arrival = jnp.take_along_axis(by_slot, targets[:, :, :, None, None], axis=2)
    return arrival.reshape(TOKENS, D)
```

```python
import functools
import math

import jax
import jax.numpy as jnp
from jax import lax
from jax.experimental import pallas as pl
from jax.experimental.pallas import tpu as pltpu
from jax.sharding import PartitionSpec as P

D = 768
HEADS = 12
HD = 64
BLK = 32
N_GROUP = 8
N_CTX = 32
N_Z = 8
N_Y = 4
TRIPLES = 4
PER = 3
QROWS = 48
ROWS = N_CTX * BLK
NEGATIVE = -1e30
SCALE = math.log2(math.e) / math.sqrt(HD)
TQ = 256
KC = 4
MESH = pl.DeviceIdType.MESH


def low_half(shape):
    return lax.broadcasted_iota(jnp.int32, shape, len(shape) - 1) < HD


def swap(x):
    return pltpu.roll(x, HD, 1)


def join(a, b):
    return jnp.where(low_half(a.shape), a, b)


def masked_rows(series_ref, recon_ref, token_ref):
    return jnp.where(
        recon_ref[...] == 1, token_ref[...].astype(jnp.float32), series_ref[...].astype(jnp.float32)
    )


def project_kernel(
    packing_ref, series_ref, recon_ref, token_ref, doc_ref, gain_ref, wq_ref, wk_ref, wv_ref,
    kv_ref, q_ref, count_ref,
):
    x = masked_rows(series_ref, recon_ref, token_ref)
    factor = lax.rsqrt(jnp.mean(x * x, axis=-1, keepdims=True) + 1e-06)
    normed = (x * factor * gain_ref[...].astype(jnp.float32)).astype(jnp.bfloat16)
    ids = doc_ref[...]
    lane = lax.broadcasted_iota(jnp.int32, (8, 128), 1)
    count = jnp.zeros((8, 128), jnp.int32)
    for d in range(3):
        below = jnp.sum((ids <= d).astype(jnp.float32), axis=1, keepdims=True).astype(jnp.int32)
        count = jnp.where(lane == d, below, count)
    count_ref[...] = count

    def project(w_ref):
        return jnp.dot(normed, w_ref[...], preferred_element_type=jnp.float32)

    def piece(values, k):
        return values[k * BLK : (k + 1) * BLK]

    key, value = project(wk_ref), project(wv_ref)
    for m in range(HEADS // 2):
        kp, vp = key[:, m * 128 : (m + 1) * 128], value[:, m * 128 : (m + 1) * 128]
        for head, kv in ((2 * m, join(kp, swap(vp))), (2 * m + 1, join(swap(kp), vp))):
            kv = kv.astype(jnp.bfloat16)
            for k in range(N_GROUP):
                kv_ref[packing_ref[k] * TRIPLES + head // PER, head % PER] = piece(kv, k)
    query = project(wq_ref) * SCALE
    for t in range(TRIPLES):
        pair = [query[:, m * 128 : (m + 1) * 128] for m in (3 * t // 2, 3 * t // 2 + 1)]
        if t % 2 == 0:
            first, last = pair[0], pair[1]
        else:
            first, last = join(swap(pair[0]), swap(pair[1])), swap(pair[1])
        first = first.astype(jnp.bfloat16)
        swapped = swap(last)
        for k in range(N_GROUP):
            to = packing_ref[k] * TRIPLES + t
            q_ref[to, 0:BLK] = piece(first, k)
            half = join(last[k * BLK : k * BLK + 16], swapped[k * BLK + 16 : (k + 1) * BLK])
            q_ref[to, BLK:QROWS] = half.astype(jnp.bfloat16)


def project(series, recon, token, packing, docs, gain, wq, wk, wv):
    vmem = pl.BlockSpec(memory_space=pltpu.VMEM)
    return pl.pallas_call(
        project_kernel,
        out_shape=(
            jax.ShapeDtypeStruct((N_CTX, PER, BLK, 128), jnp.bfloat16),
            jax.ShapeDtypeStruct((N_CTX, QROWS, 128), jnp.bfloat16),
            jax.ShapeDtypeStruct((8, 128), jnp.int32),
        ),
        in_specs=[pl.BlockSpec(memory_space=pltpu.SMEM)] + [vmem] * 8,
        out_specs=(vmem, vmem, vmem),
        compiler_params=pltpu.CompilerParams(vmem_limit_bytes=48 << 20),
        name="project",
    )(packing, series, recon, token, docs, gain, wq, wk, wv)


def step_z(i):
    return lax.rem(N_Z + (1 - 2 * lax.rem(i + 1, 2)) * ((i + 1) // 2), N_Z)


def spread_kernel(
    kv_ref, q_ref, count_ref, all_ref, qout_ref, total_ref,
    counts, kv_send, kv_recv, q_send, q_recv, c_send, c_recv, self_sem,
    x_send, near_recv, half_recv, pair_recv, t_send, t_recv,
):
    s = lax.axis_index("group")
    c = lax.axis_index("ctx")
    z, y = c // N_Y, lax.rem(c, N_Y)
    partner = s + 1 - 2 * lax.rem(s, 2)
    right, left, across = lax.rem(s + 2, N_GROUP), lax.rem(s + 6, N_GROUP), lax.rem(s + 4, N_GROUP)
    bar = pltpu.get_barrier_semaphore()

    def greet(o, carry):
        pl.semaphore_signal(
            bar, inc=1, device_id=(s, lax.rem(c + o, N_CTX)), device_id_type=MESH
        )
        return carry

    lax.fori_loop(1, N_CTX, greet, 0)
    for other in (partner, right, left):
        pl.semaphore_signal(bar, inc=1, device_id=(other, c), device_id_type=MESH)
    pl.semaphore_wait(bar, N_CTX - 1 + 3)

    def rows_of(d):
        return pl.ds(pl.multiple_of(d * BLK, BLK), BLK)

    def send_kv(d):
        return pltpu.make_async_remote_copy(
            src_ref=kv_ref.at[d], dst_ref=all_ref.at[:, s, rows_of(c), :],
            send_sem=kv_send.at[d], recv_sem=kv_recv.at[c],
            device_id=(s, d), device_id_type=MESH,
        )

    def arrive_kv(d):
        return pltpu.make_async_remote_copy(
            src_ref=kv_ref.at[d], dst_ref=all_ref.at[:, s, rows_of(d), :],
            send_sem=kv_send.at[d], recv_sem=kv_recv.at[d],
            device_id=(s, d), device_id_type=MESH,
        )

    def send_q(d, at):
        return pltpu.make_async_remote_copy(
            src_ref=q_ref.at[d], dst_ref=qout_ref.at[at],
            send_sem=q_send.at[d], recv_sem=q_recv.at[at],
            device_id=(s, d), device_id_type=MESH,
        )

    def send_count(d, at):
        return pltpu.make_async_remote_copy(
            src_ref=count_ref, dst_ref=counts.at[at],
            send_sem=c_send.at[d], recv_sem=c_recv.at[at],
            device_id=(s, d), device_id_type=MESH,
        )

    def other(i, yy):
        return lax.rem(z + step_z(i), N_Z) * N_Y + lax.rem(y + yy, N_Y)

    own_kv = pltpu.make_async_copy(kv_ref.at[c], all_ref.at[:, s, rows_of(c), :], self_sem.at[0])
    own_q = pltpu.make_async_copy(q_ref.at[c], qout_ref.at[c], self_sem.at[1])
    own_count = pltpu.make_async_copy(count_ref, counts.at[c], self_sem.at[2])
    own_kv.start()
    own_q.start()
    own_count.start()
    for yy in range(1, N_Y):
        send_kv(other(0, yy)).start()

    def start_plane(i, carry):
        for yy in range(N_Y):
            send_kv(other(i, yy)).start()
        return carry

    lax.fori_loop(1, N_Z, start_plane, 0)

    def start_rest(o, carry):
        d = lax.rem(c + o, N_CTX)
        send_count(d, c).start()
        send_q(d, c).start()
        return carry

    lax.fori_loop(1, N_CTX, start_rest, 0)

    def plane(i):
        return lax.rem(z + N_Z - step_z(i), N_Z)

    def hop(slot, i, to, kind, recv, half=None):
        first, size = plane(i) * 128, 128
        if half is not None:
            first, size = first + half * 64, 64
        part = all_ref.at[:, slot, pl.ds(pl.multiple_of(first, 64), size), :]
        return pltpu.make_async_remote_copy(
            src_ref=part, dst_ref=part, send_sem=x_send.at[kind, i], recv_sem=recv,
            device_id=(to, c), device_id_type=MESH,
        )

    def own_right(i):
        return hop(s, i, right, 0, near_recv.at[0, i])

    def own_left(i):
        return hop(s, i, left, 1, near_recv.at[1, i])

    def own_pair(i):
        return hop(s, i, partner, 2, pair_recv.at[0, i])

    def left_on(i):
        return hop(left, i, right, 3, half_recv.at[0, i], half=0)

    def right_on(i):
        return hop(right, i, left, 4, half_recv.at[1, i], half=1)

    def left_pair(i):
        return hop(left, i, partner, 5, pair_recv.at[1, i])

    def right_pair(i):
        return hop(right, i, partner, 6, pair_recv.at[2, i])

    def across_pair(i):
        return hop(across, i, partner, 7, pair_recv.at[3, i])

    def from_left(i):
        return hop(left, i, left, 0, near_recv.at[0, i])

    def from_right(i):
        return hop(right, i, right, 1, near_recv.at[1, i])

    def across_from_left(i):
        return hop(across, i, left, 3, half_recv.at[0, i], half=0)

    def across_from_right(i):
        return hop(across, i, right, 4, half_recv.at[1, i], half=1)

    def send_own(i):
        own_right(i).start()
        own_left(i).start()
        own_pair(i).start()

    def send_near(i):
        from_left(i).wait_recv()
        left_on(i).start()
        left_pair(i).start()
        from_right(i).wait_recv()
        right_on(i).start()
        right_pair(i).start()

    def send_across(i):
        across_from_left(i).wait_recv()
        across_from_right(i).wait_recv()
        across_pair(i).start()

    own_kv.wait()
    for yy in range(1, N_Y):
        arrive_kv(z * N_Y + lax.rem(y + yy, N_Y)).wait_recv()
    send_own(0)

    def arrive_plane(i):
        for yy in range(N_Y):
            arrive_kv(plane(i) * N_Y + yy).wait_recv()

    arrive_plane(1)
    send_own(1)
    send_near(0)

    def step(i, carry):
        arrive_plane(i)
        send_own(i)
        send_near(i - 1)
        send_across(i - 2)
        return carry

    lax.fori_loop(2, N_Z, step, 0)
    send_near(N_Z - 1)
    send_across(N_Z - 2)

    own_count.wait()

    def arrive_count(o, carry):
        send_count(lax.rem(c + o, N_CTX), lax.rem(c + o, N_CTX)).wait_recv()
        return carry

    lax.fori_loop(1, N_CTX, arrive_count, 0)
    total_ref[s] = jnp.sum(counts[...], axis=0)

    def pass_total(slot, to, kind):
        return pltpu.make_async_remote_copy(
            src_ref=total_ref.at[slot], dst_ref=total_ref.at[slot],
            send_sem=t_send.at[kind], recv_sem=t_recv.at[kind],
            device_id=(to, c), device_id_type=MESH,
        )

    sends = [pass_total(s, right, 0), pass_total(s, left, 1), pass_total(s, partner, 2)]
    for one in sends:
        one.start()
    send_across(N_Z - 1)
    pass_total(left, left, 0).wait_recv()
    later = [pass_total(left, right, 3), pass_total(left, partner, 4)]
    pass_total(right, right, 1).wait_recv()
    later.append(pass_total(right, partner, 5))
    for one in later:
        one.start()
    pass_total(across, left, 3).wait_recv()
    last = pass_total(across, partner, 6)
    last.start()
    back = lax.rem(partner + 6, N_GROUP)
    ahead = lax.rem(partner + 2, N_GROUP)
    beyond = lax.rem(partner + 4, N_GROUP)
    pass_total(partner, partner, 2).wait_recv()
    pass_total(back, partner, 4).wait_recv()
    pass_total(ahead, partner, 5).wait_recv()
    pass_total(beyond, partner, 6).wait_recv()
    for one in sends + later + [last]:
        one.wait_send()

    own_q.wait()

    def finish(o, carry):
        d = lax.rem(c + o, N_CTX)
        send_q(d, d).wait_recv()
        send_q(d, c).wait_send()
        send_count(d, c).wait_send()
        send_kv(d).wait_send()
        return carry

    lax.fori_loop(1, N_CTX, finish, 0)

    def finish_hops(i, carry):
        for sent in (own_right, own_left, own_pair, left_on, right_on, left_pair, right_pair, across_pair):
            sent(i).wait_send()
        for n, slot in enumerate((partner, back, ahead, beyond)):
            hop(slot, i, partner, 2, pair_recv.at[n, i]).wait_recv()
        return carry

    lax.fori_loop(0, N_Z, finish_hops, 0)


def spread(kv, q, count):
    anywhere = pl.BlockSpec(memory_space=pl.ANY)
    vmem = pl.BlockSpec(memory_space=pltpu.VMEM)
    dma = pltpu.SemaphoreType.DMA
    return pl.pallas_call(
        spread_kernel,
        out_shape=(
            jax.ShapeDtypeStruct((PER, N_GROUP, ROWS, 128), jnp.bfloat16),
            jax.ShapeDtypeStruct((N_CTX, QROWS, 128), jnp.bfloat16),
            jax.ShapeDtypeStruct((N_GROUP, 8, 128), jnp.int32),
        ),
        in_specs=[anywhere, anywhere, vmem],
        out_specs=(anywhere, anywhere, vmem),
        scratch_shapes=[
            pltpu.VMEM((N_CTX, 8, 128), jnp.int32),
            dma((N_CTX,)), dma((N_CTX,)), dma((N_CTX,)), dma((N_CTX,)), dma((N_CTX,)), dma((N_CTX,)),
            dma((3,)), dma((8, N_Z)), dma((2, N_Z)), dma((2, N_Z)), dma((4, N_Z)), dma((7,)), dma((7,)),
        ],
        compiler_params=pltpu.CompilerParams(collective_id=0, has_side_effects=True),
        name="spread",
    )(kv, q, count)


def attend_kernel(total_ref, q_ref, kv_ref, out_ref, qs, v1):
    h = pl.program_id(0)
    s = lax.axis_index("group")
    g = lax.axis_index("ctx") // N_Y
    starts = [total_ref[g, 0, d] for d in range(3)]
    zero = jnp.zeros((), jnp.float32)

    @pl.when(h == 0)
    def _():
        q = q_ref[:, 0:BLK, :].reshape(ROWS, 128).astype(jnp.float32)
        qs[...] = join(q, zero).astype(jnp.bfloat16).reshape(N_CTX, BLK, 128)

    @pl.when(h == 1)
    def _():
        q = q_ref[:, 0:BLK, :].reshape(ROWS, 128).astype(jnp.float32)
        qs[...] = join(swap(q), zero).astype(jnp.bfloat16).reshape(N_CTX, BLK, 128)

    @pl.when(h == 2)
    def _():
        q = q_ref[:, BLK:QROWS, :].reshape(ROWS // 2, 128).astype(jnp.float32)
        qs[:, 0:16] = join(q, zero).astype(jnp.bfloat16).reshape(N_CTX, 16, 128)
        qs[:, 16:32] = join(swap(q), zero).astype(jnp.bfloat16).reshape(N_CTX, 16, 128)

    one = jnp.ones((), jnp.bfloat16)
    for n in range(N_GROUP):
        v1[n] = jnp.where(low_half((ROWS, 128)), one, kv_ref[0, n])

    span = TQ // BLK * 256
    keys_n = KC * 256

    def doc_of(pos):
        return sum((pos >= st).astype(jnp.int32) for st in starts)

    for t in range(ROWS // TQ):
        p0, p1 = t * span, (t + 1) * span - 1
        lo, single, hi = jnp.int32(0), jnp.int32(0), jnp.int32(N_CTX * 256)
        for st in starts:
            lo = jnp.maximum(lo, jnp.where(st <= p0, st, 0))
            single = jnp.maximum(single, jnp.where(st <= p1, st, 0))
            hi = jnp.minimum(hi, jnp.where(st > p1, st, N_CTX * 256))
        blocks = TQ // BLK
        qt = qs[t * blocks : (t + 1) * blocks].reshape(TQ, 128)
        i = lax.broadcasted_iota(jnp.int32, (TQ, 1), 0)
        q_doc = doc_of((t * blocks + i // BLK) * 256 + s * BLK + i % BLK)

        def tile(kb, carry, masked):
            m, acc = carry
            rows = pl.ds(pl.multiple_of(kb * (KC * BLK), KC * BLK), KC * BLK)
            keys = kv_ref[0, :, rows, :].reshape(keys_n, 128)
            sc = lax.dot_general(
                qt, keys, (((1,), (1,)), ((), ())), preferred_element_type=jnp.float32
            )
            if masked:
                r = lax.broadcasted_iota(jnp.int32, (1, keys_n), 1)
                at = r % (KC * BLK)
                pos = (kb * KC + at // BLK) * 256 + (r // (KC * BLK)) * BLK + at % BLK
                sc = jnp.where(q_doc == doc_of(pos), sc, NEGATIVE)
            new = jnp.maximum(m, jnp.max(sc, axis=1, keepdims=True))
            p = jnp.exp2(sc - new).astype(jnp.bfloat16)
            acc = acc * jnp.exp2(m - new) + jnp.dot(
                p, v1[:, rows, :].reshape(keys_n, 128), preferred_element_type=jnp.float32
            )
            return new, acc

        def body(kb, carry):
            clear = (lo == single) & (kb * keys_n >= lo) & ((kb + 1) * keys_n <= hi)
            return lax.cond(
                clear,
                lambda: tile(kb, carry, False),
                lambda: tile(kb, carry, True),
            )

        m, acc = lax.fori_loop(
            lo // keys_n,
            (hi + keys_n - 1) // keys_n,
            body,
            (jnp.full((TQ, 1), NEGATIVE, jnp.float32), jnp.zeros((TQ, 128), jnp.float32)),
        )
        o = acc / swap(acc)

        here = slice(t * blocks, (t + 1) * blocks)

        @pl.when(h == 0)
        def _():
            out_ref[here, 0:BLK] = swap(o).astype(jnp.bfloat16).reshape(blocks, BLK, 128)

        @pl.when(h == 1)
        def _():
            before = out_ref[here, 0:BLK].reshape(TQ, 128)
            out_ref[here, 0:BLK] = join(before, o.astype(jnp.bfloat16)).reshape(blocks, BLK, 128)

        @pl.when(h == 2)
        def _():
            o3 = o.reshape(blocks, BLK, 128)
            first, second = o3[:, 0:16].reshape(TQ // 2, 128), o3[:, 16:32].reshape(TQ // 2, 128)
            both = join(swap(first), second).astype(jnp.bfloat16)
            out_ref[here, BLK:QROWS] = both.reshape(blocks, 16, 128)


def attend(total, q, kv):
    return pl.pallas_call(
        attend_kernel,
        out_shape=jax.ShapeDtypeStruct((N_CTX, QROWS, 128), jnp.bfloat16),
        grid=(PER,),
        in_specs=[
            pl.BlockSpec(memory_space=pltpu.SMEM),
            pl.BlockSpec((N_CTX, QROWS, 128), lambda h: (0, 0, 0)),
            pl.BlockSpec((1, N_GROUP, ROWS, 128), lambda h: (h, 0, 0, 0)),
        ],
        out_specs=pl.BlockSpec((N_CTX, QROWS, 128), lambda h: (0, 0, 0)),
        scratch_shapes=[
            pltpu.VMEM((N_CTX, BLK, 128), jnp.bfloat16),
            pltpu.VMEM((N_GROUP, ROWS, 128), jnp.bfloat16),
        ],
        compiler_params=pltpu.CompilerParams(
            vmem_limit_bytes=56 << 20, dimension_semantics=("arbitrary",)
        ),
        name="attend",
    )(total, q, kv)


def finish_kernel(packing_ref, att_ref, series_ref, recon_ref, token_ref, w_ref, out_ref, lhs, w2):
    order = [PER * t + n for t in range(TRIPLES) for n in range(2)] + [2, 5, 8, 11]
    for n, head in enumerate(order):
        w2[n * HD : (n + 1) * HD, :] = w_ref[head * HD : (head + 1) * HD, :]
    for k in range(N_GROUP):
        g = packing_ref[k]
        rows = slice(k * BLK, (k + 1) * BLK)
        for t in range(TRIPLES):
            lhs[rows, t * 128 : (t + 1) * 128] = att_ref[g * TRIPLES + t, 0:BLK]
        for n in range(2):
            a = att_ref[g * TRIPLES + 2 * n, BLK:QROWS].astype(jnp.float32)
            b = att_ref[g * TRIPLES + 2 * n + 1, BLK:QROWS].astype(jnp.float32)
            cols = slice((TRIPLES + n) * 128, (TRIPLES + n + 1) * 128)
            lhs[k * BLK : k * BLK + 16, cols] = join(a, swap(b)).astype(jnp.bfloat16)
            lhs[k * BLK + 16 : (k + 1) * BLK, cols] = join(swap(a), b).astype(jnp.bfloat16)
    mixed = jnp.dot(lhs[...], w2[...], preferred_element_type=jnp.float32)
    out_ref[...] = (masked_rows(series_ref, recon_ref, token_ref) + mixed).astype(jnp.bfloat16)


def finish(packing, att, series, recon, token, w_out):
    vmem = pl.BlockSpec(memory_space=pltpu.VMEM)
    return pl.pallas_call(
        finish_kernel,
        out_shape=jax.ShapeDtypeStruct(series.shape, jnp.bfloat16),
        in_specs=[pl.BlockSpec(memory_space=pltpu.SMEM)] + [vmem] * 5,
        out_specs=vmem,
        scratch_shapes=[pltpu.VMEM((N_GROUP * BLK, D), jnp.bfloat16), pltpu.VMEM((D, D), jnp.bfloat16)],
        compiler_params=pltpu.CompilerParams(vmem_limit_bytes=48 << 20),
        name="finish",
    )(packing, att, series, recon, token, w_out)


def on_device(
    series, recon_mask, mask_token, packing_list, doc_ids, norm_gain, w_query, w_key, w_value, w_out
):
    recon = recon_mask.reshape(-1, 1)
    token = mask_token.reshape(1, -1)
    kv, q, count = project(
        series, recon, token, packing_list, doc_ids, norm_gain.reshape(1, -1), w_query, w_key, w_value
    )
    all_kv, q_rows, total = spread(kv, q, count)
    att = attend(total, q_rows, all_kv)
    back = lax.all_to_all(att, "ctx", split_axis=0, concat_axis=0, tiled=True)
    return finish(packing_list, back, series, recon, token, w_out)


def solution(mesh):
    split = P(("group", "ctx"))
    in_specs = (
        P(("group", "ctx"), None), split, P(), split, P("group", "ctx"), P(), P(), P(), P(), P(),
    )
    return jax.shard_map(
        on_device, mesh=mesh, in_specs=in_specs, out_specs=P(("group", "ctx"), None), check_vma=False
    )
```

```python
import functools
import math

import jax
import jax.numpy as jnp
from jax import lax
from jax.experimental import pallas as pl
from jax.experimental.pallas import tpu as pltpu
from jax.sharding import PartitionSpec as P

D = 768
HEADS = 12
HD = 64
BLK = 32
N_GROUP = 8
N_CTX = 32
N_Z = 8
N_Y = 4
TRIPLES = 4
PER = 3
QROWS = 48
ROWS = N_CTX * BLK
NEGATIVE = -1e30
DOCS = 4
BOUND = 100.0
SCALE = math.log2(math.e) / math.sqrt(HD)
TQ = 256
KC = 4
MESH = pl.DeviceIdType.MESH


def low_half(shape):
    return lax.broadcasted_iota(jnp.int32, shape, len(shape) - 1) < HD


def swap(x):
    return pltpu.roll(x, HD, 1)


def join(a, b):
    return jnp.where(low_half(a.shape), a, b)


def masked_rows(series_ref, recon_ref, token_ref):
    return jnp.where(
        recon_ref[...] == 1, token_ref[...].astype(jnp.float32), series_ref[...].astype(jnp.float32)
    )


def project_kernel(
    packing_ref, series_ref, recon_ref, token_ref, doc_ref, gain_ref, wq_ref, wk_ref, wv_ref,
    kv_ref, q_ref, count_ref,
):
    x = masked_rows(series_ref, recon_ref, token_ref)
    factor = lax.rsqrt(jnp.mean(x * x, axis=-1, keepdims=True) + 1e-06)
    normed = (x * factor * gain_ref[...].astype(jnp.float32)).astype(jnp.bfloat16)
    ids = doc_ref[...]
    lane = lax.broadcasted_iota(jnp.int32, (8, 128), 1)
    count = jnp.zeros((8, 128), jnp.int32)
    for d in range(3):
        below = jnp.sum((ids <= d).astype(jnp.float32), axis=1, keepdims=True).astype(jnp.int32)
        count = jnp.where(lane == d, below, count)

    def project(w_ref):
        return jnp.dot(normed, w_ref[...], preferred_element_type=jnp.float32)

    def piece(values, k):
        return values[k * BLK : (k + 1) * BLK]

    key, value = project(wk_ref), project(wv_ref)
    for m in range(HEADS // 2):
        kp, vp = key[:, m * 128 : (m + 1) * 128], value[:, m * 128 : (m + 1) * 128]
        for head, kv in ((2 * m, join(kp, swap(vp))), (2 * m + 1, join(swap(kp), vp))):
            kv = kv.astype(jnp.bfloat16)
            for k in range(N_GROUP):
                kv_ref[packing_ref[k] * TRIPLES + head // PER, head % PER] = piece(kv, k)
    query = project(wq_ref) * SCALE
    for t in range(TRIPLES):
        pair = [query[:, m * 128 : (m + 1) * 128] for m in (3 * t // 2, 3 * t // 2 + 1)]
        if t % 2 == 0:
            first, last = pair[0], pair[1]
        else:
            first, last = join(swap(pair[0]), swap(pair[1])), swap(pair[1])
        first = first.astype(jnp.bfloat16)
        swapped = swap(last)
        for k in range(N_GROUP):
            to = packing_ref[k] * TRIPLES + t
            q_ref[to, 0:BLK] = piece(first, k)
            half = join(last[k * BLK : k * BLK + 16], swapped[k * BLK + 16 : (k + 1) * BLK])
            q_ref[to, BLK:QROWS] = half.astype(jnp.bfloat16)


    count_ref[...] = count


def project(series, recon, token, packing, docs, gain, wq, wk, wv):
    vmem = pl.BlockSpec(memory_space=pltpu.VMEM)
    return pl.pallas_call(
        project_kernel,
        out_shape=(
            jax.ShapeDtypeStruct((N_CTX, PER, BLK, 128), jnp.bfloat16),
            jax.ShapeDtypeStruct((N_CTX, QROWS, 128), jnp.bfloat16),
            jax.ShapeDtypeStruct((8, 128), jnp.int32),
        ),
        in_specs=[pl.BlockSpec(memory_space=pltpu.SMEM)] + [vmem] * 8,
        out_specs=(vmem, vmem, vmem),
        compiler_params=pltpu.CompilerParams(vmem_limit_bytes=48 << 20),
        name="project",
    )(packing, series, recon, token, docs, gain, wq, wk, wv)


def step_z(i):
    return lax.rem(N_Z + (1 - 2 * lax.rem(i + 1, 2)) * ((i + 1) // 2), N_Z)


def spread_kernel(
    kv_ref, q_ref, count_ref, all_ref, qout_ref, total_ref,
    counts, kv_send, kv_recv, q_send, q_recv, c_send, c_recv, self_sem,
    x_send, near_recv, half_recv, pair_recv, t_send, t_recv,
):
    s = lax.axis_index("group")
    c = lax.axis_index("ctx")
    z, y = c // N_Y, lax.rem(c, N_Y)
    partner = s + 1 - 2 * lax.rem(s, 2)
    right, left, across = lax.rem(s + 2, N_GROUP), lax.rem(s + 6, N_GROUP), lax.rem(s + 4, N_GROUP)
    owner = z == s
    bar = pltpu.get_barrier_semaphore()

    def greet(o, carry):
        pl.semaphore_signal(bar, inc=1, device_id=(s, lax.rem(c + o, N_CTX)), device_id_type=MESH)
        return carry

    lax.fori_loop(1, N_CTX, greet, 0)
    for o in range(1, N_GROUP):
        pl.semaphore_signal(bar, inc=1, device_id=(lax.rem(s + o, N_GROUP), c), device_id_type=MESH)
    pl.semaphore_wait(bar, N_CTX - 1 + N_GROUP - 1)

    def rows_of(d):
        return pl.ds(pl.multiple_of(d * BLK, BLK), BLK)

    def send_kv(d, i):
        return pltpu.make_async_remote_copy(
            src_ref=kv_ref.at[d], dst_ref=all_ref.at[:, s, rows_of(c), :],
            send_sem=kv_send, recv_sem=kv_recv.at[i],
            device_id=(s, d), device_id_type=MESH,
        )

    def send_q(d):
        return pltpu.make_async_remote_copy(
            src_ref=q_ref.at[d], dst_ref=qout_ref.at[c], send_sem=q_send, recv_sem=q_recv,
            device_id=(s, d), device_id_type=MESH,
        )

    def send_count(t):
        return pltpu.make_async_remote_copy(
            src_ref=count_ref, dst_ref=counts.at[c], send_sem=c_send.at[t], recv_sem=c_recv,
            device_id=(s, s * N_Y + t), device_id_type=MESH,
        )

    def send_total(o):
        return pltpu.make_async_remote_copy(
            src_ref=total_ref, dst_ref=total_ref, send_sem=t_send.at[o - 1], recv_sem=t_recv,
            device_id=(lax.rem(s + o, N_GROUP), c), device_id_type=MESH,
        )

    def other(i, yy):
        return lax.rem(z + step_z(i), N_Z) * N_Y + lax.rem(y + yy, N_Y)

    own_kv = pltpu.make_async_copy(kv_ref.at[c], all_ref.at[:, s, rows_of(c), :], self_sem.at[0])
    own_q = pltpu.make_async_copy(q_ref.at[c], qout_ref.at[c], self_sem.at[1])
    own_kv.start()
    for yy in range(1, N_Y):
        send_kv(other(0, yy), 0).start()

    def start_plane(i, carry):
        for yy in range(N_Y):
            send_kv(other(i, yy), i).start()
        return carry

    lax.fori_loop(1, 3, start_plane, 0)
    for t in range(N_Y):
        @pl.when(s * N_Y + t != c)
        def _():
            send_count(t).start()

    lax.fori_loop(3, N_Z, start_plane, 0)
    own_q.start()

    def start_q(i, carry):
        for yy in range(N_Y):
            send_q(other(i, yy)).start()
        return carry

    for yy in range(1, N_Y):
        send_q(other(0, yy)).start()
    lax.fori_loop(1, N_Z, start_q, 0)

    def plane(i):
        return lax.rem(z + N_Z - step_z(i), N_Z)

    def hop(slot, i, to, kind, recv, half=None):
        first, size = plane(i) * 128, 128
        if half is not None:
            first, size = first + half * 64, 64
        part = all_ref.at[:, slot, pl.ds(pl.multiple_of(first, 64), size), :]
        return pltpu.make_async_remote_copy(
            src_ref=part, dst_ref=part, send_sem=x_send.at[kind], recv_sem=recv,
            device_id=(to, c), device_id_type=MESH,
        )

    def whole(slot, kind, recv, half=None):
        part = all_ref.at[:, slot, pl.ds(0, ROWS if half is None else ROWS // 2), :]
        return pltpu.make_async_remote_copy(
            src_ref=part, dst_ref=part, send_sem=x_send.at[kind], recv_sem=recv,
            device_id=(partner, c), device_id_type=MESH,
        )

    def send_own(i):
        hop(s, i, right, 0, near_recv.at[0, i]).start()
        hop(s, i, left, 1, near_recv.at[1, i]).start()
        hop(s, i, partner, 2, pair_recv.at[0]).start()

    def send_near(i):
        hop(left, i, left, 0, near_recv.at[0, i]).wait_recv()
        hop(left, i, right, 3, half_recv.at[0, i], half=0).start()
        hop(left, i, partner, 5, pair_recv.at[1]).start()
        hop(right, i, right, 1, near_recv.at[1, i]).wait_recv()
        hop(right, i, left, 4, half_recv.at[1, i], half=1).start()
        hop(right, i, partner, 6, pair_recv.at[2]).start()

    def send_across(i):
        hop(across, i, left, 3, half_recv.at[0, i], half=0).wait_recv()
        hop(across, i, right, 4, half_recv.at[1, i], half=1).wait_recv()
        hop(across, i, partner, 7, pair_recv.at[3]).start()

    def arrive_plane(i):
        part = all_ref.at[:, s, pl.ds(pl.multiple_of(plane(i) * 128, 128), 128), :]
        pltpu.make_async_remote_copy(
            src_ref=part, dst_ref=part, send_sem=kv_send, recv_sem=kv_recv.at[i],
            device_id=(partner, c), device_id_type=MESH,
        ).wait_recv()

    own_kv.wait()
    three = all_ref.at[:, s, pl.ds(pl.multiple_of(z * 128, 128), 96), :]
    pltpu.make_async_remote_copy(
        src_ref=three, dst_ref=three, send_sem=kv_send, recv_sem=kv_recv.at[0],
        device_id=(partner, c), device_id_type=MESH,
    ).wait_recv()
    send_own(0)
    arrive_plane(1)
    send_own(1)
    send_near(0)

    def step(i, carry):
        arrive_plane(i)
        send_own(i)
        send_near(i - 1)
        send_across(i - 2)
        return carry

    lax.fori_loop(2, 5, step, 0)

    @pl.when(owner)
    def _():
        counts[c] = count_ref[...]
        rest = counts.at[pl.ds(0, N_CTX - 1)]
        pltpu.make_async_remote_copy(
            src_ref=rest, dst_ref=rest, send_sem=c_send.at[0], recv_sem=c_recv,
            device_id=(partner, c), device_id_type=MESH,
        ).wait_recv()
        total_ref[...] = jnp.sum(counts[...], axis=0)
        for o in range(1, N_GROUP):
            send_total(o).start()

    lax.fori_loop(5, N_Z, step, 0)
    send_near(N_Z - 1)
    send_across(N_Z - 2)
    send_across(N_Z - 1)

    for t in range(N_Y):
        @pl.when(s * N_Y + t != c)
        def _():
            send_count(t).wait_send()

    @pl.when(owner)
    def _():
        for o in range(1, N_GROUP):
            send_total(o).wait_send()

    @pl.when(jnp.logical_not(owner))
    def _():
        send_total(1).wait_recv()

    own_q.wait()
    rest = pltpu.make_async_remote_copy(
        src_ref=q_ref.at[pl.ds(0, N_CTX - 1)], dst_ref=qout_ref.at[pl.ds(0, N_CTX - 1)],
        send_sem=q_send, recv_sem=q_recv, device_id=(partner, c), device_id_type=MESH,
    )
    rest.wait_recv()
    rest.wait_send()
    sent = kv_ref.at[pl.ds(0, N_CTX - 1)]
    pltpu.make_async_remote_copy(
        src_ref=sent, dst_ref=sent, send_sem=kv_send, recv_sem=kv_recv.at[0],
        device_id=(partner, c), device_id_type=MESH,
    ).wait_send()
    for kind, slot in enumerate((s, s, s, left, right, left, right, across)):
        whole(slot, kind, t_recv, half=0 if kind in (3, 4) else None).wait_send()
    slots = (partner, lax.rem(partner + 6, N_GROUP), lax.rem(partner + 2, N_GROUP), lax.rem(partner + 4, N_GROUP))
    for n, slot in enumerate(slots):
        whole(slot, 2, pair_recv.at[n]).wait_recv()


def spread(kv, q, count):
    anywhere = pl.BlockSpec(memory_space=pl.ANY)
    vmem = pl.BlockSpec(memory_space=pltpu.VMEM)
    dma = pltpu.SemaphoreType.DMA
    return pl.pallas_call(
        spread_kernel,
        out_shape=(
            jax.ShapeDtypeStruct((PER, N_GROUP, ROWS, 128), jnp.bfloat16),
            jax.ShapeDtypeStruct((N_CTX, QROWS, 128), jnp.bfloat16),
            jax.ShapeDtypeStruct((8, 128), jnp.int32),
        ),
        in_specs=[anywhere, anywhere, vmem],
        out_specs=(anywhere, anywhere, vmem),
        scratch_shapes=[
            pltpu.VMEM((N_CTX, 8, 128), jnp.int32),
            dma(()), dma((N_Z,)), dma(()), dma(()), dma((N_Y,)), dma(()), dma((2,)),
            dma((8,)), dma((2, N_Z)), dma((2, N_Z)), dma((4,)), dma((N_GROUP - 1,)), dma(()),
        ],
        compiler_params=pltpu.CompilerParams(collective_id=0, has_side_effects=True),
        name="spread",
    )(kv, q, count)


def attend_kernel(total_ref, q_ref, kv_ref, out_ref, kv, qt, k1, vt, acc, top, sem):
    s = lax.axis_index("group")
    copies = [pltpu.make_async_copy(kv_ref.at[h], kv.at[h], sem.at[h]) for h in range(PER)]
    for copy in copies:
        copy.start()
    starts = [total_ref[0, d] for d in range(3)]
    first, last = [jnp.int32(0)] + starts, starts + [jnp.int32(N_CTX * 256)]

    def edges(index):
        lo, hi = jnp.full(index.shape, N_CTX * 256), jnp.zeros(index.shape, jnp.int32)
        for d in range(DOCS):
            lo = jnp.where(index == HD + d, first[d], lo)
            hi = jnp.where(index == HD + d, last[d], hi)
        return lo, hi

    col = lax.broadcasted_iota(jnp.int32, (1, ROWS), 1)
    pos = (col // BLK) * 256 + s * BLK + col % BLK
    row = lax.broadcasted_iota(jnp.int32, (HD, 1), 0) + HD
    lo, hi = edges(row)
    own = (pos >= lo) & (pos < hi)
    far = jnp.where(own | (row >= HD + DOCS), 0.0, NEGATIVE)

    a = q_ref[:, 0:BLK, :].reshape(ROWS, 128).astype(jnp.float32).T
    b = q_ref[:, BLK:QROWS, :].astype(jnp.float32)
    b = jnp.concatenate([b, swap(b.reshape(ROWS // 2, 128)).reshape(N_CTX, 16, 128)], axis=1)
    b = b.reshape(ROWS, 128).T
    q_top = []
    for h, part in enumerate((a[0:HD], a[HD:128], b[0:HD])):
        q_top.append(jnp.max(jnp.sum(part * part, axis=0, keepdims=True)))
        qt[h] = jnp.concatenate([part, far], axis=0).astype(jnp.bfloat16)

    r = lax.broadcasted_iota(jnp.int32, (ROWS, 128), 0)
    base = (r // BLK) * 256 + r % BLK
    lo, hi = edges(lax.broadcasted_iota(jnp.int32, (1, 128), 1))
    keys_n = KC * 256
    low = low_half((ROWS, 128))
    vt[:, :, 0:16, :] = jnp.ones((PER, N_CTX // KC, 16, keys_n), jnp.bfloat16)
    small = None
    for h in range(PER):
        copies[h].wait()
        for n in range(N_GROUP):
            both = kv[h, n]
            if h == 0:
                own = (base >= lo - n * BLK) & (base < hi - n * BLK)
                mark = jnp.where(own, 1.0, 0.0).astype(jnp.bfloat16)
            else:
                mark = k1[0, n]
            k1[h, n] = jnp.where(low, both, mark)
        norms = jnp.zeros((1, keys_n), jnp.float32)
        for kb in range(N_CTX // KC):
            block = kv[h, :, kb * KC * BLK : (kb + 1) * KC * BLK, :].reshape(keys_n, 128).T
            vt[h, kb, 16:80, :] = block[HD:128]
            keys = block[0:HD].astype(jnp.float32)
            norms = jnp.maximum(norms, jnp.sum(keys * keys, axis=0, keepdims=True))
        fits = q_top[h] * jnp.max(norms) * 1.05 <= BOUND * BOUND
        small = fits if small is None else small & fits

    span = TQ // BLK * 256
    blocks = TQ // BLK

    def tile(t, carry):
        p0 = t * span
        p1 = p0 + span - 1
        lo, hi = jnp.int32(0), jnp.int32(N_CTX * 256)
        for st in starts:
            lo = jnp.maximum(lo, jnp.where(st <= p0, st, 0))
            hi = jnp.minimum(hi, jnp.where(st > p1, st, N_CTX * 256))
        begin, end = lo // keys_n, (hi + keys_n - 1) // keys_n
        cols = pl.ds(pl.multiple_of(t * TQ, TQ), TQ)

        def scores(h, kb):
            rows = pl.ds(pl.multiple_of(kb * KC * BLK, KC * BLK), KC * BLK)
            keys = k1[h, :, rows, :].reshape(keys_n, 128)
            return jnp.dot(keys, qt[h, :, cols], preferred_element_type=jnp.float32)

        def summed(h, kb, p):
            return jnp.dot(vt[h, kb], p, preferred_element_type=jnp.float32)

        acc[...] = jnp.zeros_like(acc)

        @pl.when(small)
        def _():
            def body(kb, carry):
                weights = [scores(h, kb) for h in range(PER)]
                weights = [jnp.exp2(w).astype(jnp.bfloat16) for w in weights]
                sums = [summed(h, kb, weights[h]) for h in range(PER)]
                for h in range(PER):
                    acc[h] += sums[h]
                return carry

            lax.fori_loop(begin, end, body, 0)

        @pl.when(jnp.logical_not(small))
        def _():
            top[...] = jnp.full_like(top, NEGATIVE)

            def body(kb, carry):
                all_scores = [scores(h, kb) for h in range(PER)]
                for h, sc in enumerate(all_scores):
                    old = top[h]
                    new = jnp.maximum(old, jnp.max(sc, axis=0, keepdims=True))
                    top[h] = new
                    weights = jnp.exp2(sc - new).astype(jnp.bfloat16)
                    acc[h] = acc[h] * jnp.exp2(old - new) + summed(h, kb, weights)
                return carry

            lax.fori_loop(begin, end, body, 0)

        def attended(h):
            return acc[h, 16:80, :] / acc[h, 0:1, :]

        here = pl.ds(t * blocks, blocks)
        o = jnp.concatenate([attended(0), attended(1)], axis=0).T
        out_ref[here, 0:BLK] = o.astype(jnp.bfloat16).reshape(blocks, BLK, 128)
        o = attended(2)
        o = jnp.concatenate([o, o], axis=0).T.reshape(blocks, BLK, 128)
        one, two = o[:, 0:16].reshape(TQ // 2, 128), o[:, 16:32].reshape(TQ // 2, 128)
        out_ref[here, BLK:QROWS] = join(one, two).astype(jnp.bfloat16).reshape(blocks, 16, 128)
        return carry

    lax.fori_loop(0, ROWS // TQ, tile, 0)


def attend(total, q, kv):
    vmem = pl.BlockSpec(memory_space=pltpu.VMEM)
    wide = pltpu.VMEM((PER, N_GROUP, ROWS, 128), jnp.bfloat16)
    return pl.pallas_call(
        attend_kernel,
        out_shape=jax.ShapeDtypeStruct((N_CTX, QROWS, 128), jnp.bfloat16),
        in_specs=[pl.BlockSpec(memory_space=pltpu.SMEM), vmem, pl.BlockSpec(memory_space=pl.ANY)],
        out_specs=vmem,
        scratch_shapes=[
            wide,
            pltpu.VMEM((PER, 128, ROWS), jnp.bfloat16),
            wide,
            pltpu.VMEM((PER, N_CTX // KC, 80, KC * 256), jnp.bfloat16),
            pltpu.VMEM((PER, 80, TQ), jnp.float32),
            pltpu.VMEM((PER, 1, TQ), jnp.float32),
            pltpu.SemaphoreType.DMA((PER,)),
        ],
        compiler_params=pltpu.CompilerParams(vmem_limit_bytes=56 << 20),
        name="attend",
    )(total, q, kv)


def finish_kernel(packing_ref, att_ref, series_ref, recon_ref, token_ref, w_ref, out_ref, lhs, w2):
    order = [PER * t + n for t in range(TRIPLES) for n in range(2)] + [2, 5, 8, 11]
    for n, head in enumerate(order):
        w2[n * HD : (n + 1) * HD, :] = w_ref[head * HD : (head + 1) * HD, :]
    for k in range(N_GROUP):
        g = packing_ref[k]
        rows = slice(k * BLK, (k + 1) * BLK)
        for t in range(TRIPLES):
            lhs[rows, t * 128 : (t + 1) * 128] = att_ref[g * TRIPLES + t, 0:BLK]
        for n in range(2):
            a = att_ref[g * TRIPLES + 2 * n, BLK:QROWS].astype(jnp.float32)
            b = att_ref[g * TRIPLES + 2 * n + 1, BLK:QROWS].astype(jnp.float32)
            cols = slice((TRIPLES + n) * 128, (TRIPLES + n + 1) * 128)
            lhs[k * BLK : k * BLK + 16, cols] = join(a, swap(b)).astype(jnp.bfloat16)
            lhs[k * BLK + 16 : (k + 1) * BLK, cols] = join(swap(a), b).astype(jnp.bfloat16)
    mixed = jnp.dot(lhs[...], w2[...], preferred_element_type=jnp.float32)
    out_ref[...] = (masked_rows(series_ref, recon_ref, token_ref) + mixed).astype(jnp.bfloat16)


def finish(packing, att, series, recon, token, w_out):
    vmem = pl.BlockSpec(memory_space=pltpu.VMEM)
    return pl.pallas_call(
        finish_kernel,
        out_shape=jax.ShapeDtypeStruct(series.shape, jnp.bfloat16),
        in_specs=[pl.BlockSpec(memory_space=pltpu.SMEM)] + [vmem] * 5,
        out_specs=vmem,
        scratch_shapes=[pltpu.VMEM((N_GROUP * BLK, D), jnp.bfloat16), pltpu.VMEM((D, D), jnp.bfloat16)],
        compiler_params=pltpu.CompilerParams(vmem_limit_bytes=48 << 20),
        name="finish",
    )(packing, att, series, recon, token, w_out)


def on_device(
    series, recon_mask, mask_token, packing_list, doc_ids, norm_gain, w_query, w_key, w_value, w_out
):
    recon = recon_mask.reshape(-1, 1)
    token = mask_token.reshape(1, -1)
    kv, q, count = project(
        series, recon, token, packing_list, doc_ids, norm_gain.reshape(1, -1), w_query, w_key, w_value
    )
    all_kv, q_rows, total = spread(kv, q, count)
    att = attend(total, q_rows, all_kv)
    back = lax.all_to_all(att, "ctx", split_axis=0, concat_axis=0, tiled=True)
    return finish(packing_list, back, series, recon, token, w_out)


def solution(mesh):
    split = P(("group", "ctx"))
    in_specs = (
        P(("group", "ctx"), None), split, P(), split, P("group", "ctx"), P(), P(), P(), P(), P(),
    )
    return jax.shard_map(
        on_device, mesh=mesh, in_specs=in_specs, out_specs=P(("group", "ctx"), None), check_vma=False
    )
```

```python
import functools
import math

import jax
import jax.numpy as jnp
from jax import lax
from jax.experimental import pallas as pl
from jax.experimental.pallas import tpu as pltpu
from jax.sharding import PartitionSpec as P

D = 768
HEADS = 12
HD = 64
BLK = 32
N_GROUP = 8
N_CTX = 32
N_Z = 8
N_Y = 4
TRIPLES = 4
PER = 3
QROWS = 48
ROWS = N_CTX * BLK
NEGATIVE = -1e30
DOCS = 4
BOUND = 100.0
SCALE = math.log2(math.e) / math.sqrt(HD)
TQ = 256
KC = 4
MESH = pl.DeviceIdType.MESH


def low_half(shape):
    return lax.broadcasted_iota(jnp.int32, shape, len(shape) - 1) < HD


def swap(x):
    return pltpu.roll(x, HD, 1)


def join(a, b):
    return jnp.where(low_half(a.shape), a, b)


def row_mask(recon_ref):
    flags = recon_ref[...].astype(jnp.float32)
    return jnp.broadcast_to(flags, (128, flags.shape[1])).T


def masked_rows(rows, flags, token_ref):
    flags = jnp.concatenate([flags] * (D // 128), axis=1)
    return jnp.where(flags == 1.0, token_ref[...].astype(jnp.float32), rows.astype(jnp.float32))


def normed_rows(packing_ref, series_ref, recon_ref, token_ref, gain_ref, flags):
    flags[...] = row_mask(recon_ref).reshape(N_GROUP, BLK, 128)
    pieces = []
    for g in range(N_GROUP):
        at = jnp.int32(0)
        for k in range(1, N_GROUP):
            at = jnp.where(packing_ref[k] == g, k, at)
        pieces.append(masked_rows(series_ref[at], flags[at], token_ref))
    x = jnp.concatenate(pieces, axis=0)
    factor = lax.rsqrt(jnp.mean(x * x, axis=-1, keepdims=True) + 1e-06)
    return (x * factor * gain_ref[...].astype(jnp.float32)).astype(jnp.bfloat16)


def document_counts(doc_ref):
    ids = doc_ref[...]
    lane = lax.broadcasted_iota(jnp.int32, (8, 128), 1)
    count = jnp.zeros((8, 128), jnp.int32)
    for d in range(DOCS - 1):
        below = jnp.sum((ids <= d).astype(jnp.float32), axis=1, keepdims=True).astype(jnp.int32)
        count = jnp.where(lane == d, below, count)
    return count


def piece(values, g):
    return values[g * BLK : (g + 1) * BLK]


def pack_keys(kv_ref, key, value):
    for m in range(HEADS // 2):
        kp, vp = key[:, m * 128 : (m + 1) * 128], value[:, m * 128 : (m + 1) * 128]
        for head, kv in ((2 * m, join(kp, swap(vp))), (2 * m + 1, join(swap(kp), vp))):
            kv = kv.astype(jnp.bfloat16)
            for g in range(N_GROUP):
                kv_ref[g * TRIPLES + head // PER, head % PER] = piece(kv, g)


def pack_queries(q_ref, query):
    for t in range(TRIPLES):
        pair = [query[:, m * 128 : (m + 1) * 128] for m in (3 * t // 2, 3 * t // 2 + 1)]
        if t % 2 == 0:
            first, last = pair[0], pair[1]
        else:
            first, last = join(swap(pair[0]), swap(pair[1])), swap(pair[1])
        first = first.astype(jnp.bfloat16)
        swapped = swap(last)
        for g in range(N_GROUP):
            to = g * TRIPLES + t
            q_ref[to, 0:BLK] = piece(first, g)
            half = join(last[g * BLK : g * BLK + 16], swapped[g * BLK + 16 : (g + 1) * BLK])
            q_ref[to, BLK:QROWS] = half.astype(jnp.bfloat16)


def step_z(i):
    return lax.rem(N_Z + (1 - 2 * lax.rem(i + 1, 2)) * ((i + 1) // 2), N_Z)


def spread_kernel(
    packing_ref, series_ref, recon_ref, token_ref, doc_ref, gain_ref, wq_ref, wk_ref, wv_ref,
    all_ref, qout_ref, total_ref,
    kv_ref, q_ref, count_ref, flags, wq, wk, wv, w_sem, counts, kv_send, kv_recv, q_send, q_recv, c_send, c_recv, self_sem,
    x_send, near_recv, half_recv, pair_recv, t_send, t_recv,
):
    s = lax.axis_index("group")
    c = lax.axis_index("ctx")
    z, y = c // N_Y, lax.rem(c, N_Y)
    partner = s + 1 - 2 * lax.rem(s, 2)
    right, left, across = lax.rem(s + 2, N_GROUP), lax.rem(s + 6, N_GROUP), lax.rem(s + 4, N_GROUP)
    owner = z == s
    bar = pltpu.get_barrier_semaphore()

    def greet(o, carry):
        pl.semaphore_signal(bar, inc=1, device_id=(s, lax.rem(c + o, N_CTX)), device_id_type=MESH)
        return carry

    lax.fori_loop(1, N_CTX, greet, 0)
    for o in range(1, N_GROUP):
        pl.semaphore_signal(bar, inc=1, device_id=(lax.rem(s + o, N_GROUP), c), device_id_type=MESH)
    loads = [
        pltpu.make_async_copy(src, dst, w_sem.at[n])
        for n, (src, dst) in enumerate(((wk_ref, wk), (wv_ref, wv), (wq_ref, wq)))
    ]
    for load in loads:
        load.start()
    count_ref[...] = document_counts(doc_ref)
    normed = normed_rows(packing_ref, series_ref, recon_ref, token_ref, gain_ref, flags)

    def project(n, w):
        loads[n].wait()
        return jnp.dot(normed, w[...], preferred_element_type=jnp.float32)

    pack_keys(kv_ref, project(0, wk), project(1, wv))
    pl.semaphore_wait(bar, N_CTX - 1 + N_GROUP - 1)

    def rows_of(d):
        return pl.ds(pl.multiple_of(d * BLK, BLK), BLK)

    def send_kv(d, i):
        return pltpu.make_async_remote_copy(
            src_ref=kv_ref.at[d], dst_ref=all_ref.at[:, s, rows_of(c), :],
            send_sem=kv_send, recv_sem=kv_recv.at[i],
            device_id=(s, d), device_id_type=MESH,
        )

    def send_q(d):
        return pltpu.make_async_remote_copy(
            src_ref=q_ref.at[d], dst_ref=qout_ref.at[c], send_sem=q_send, recv_sem=q_recv,
            device_id=(s, d), device_id_type=MESH,
        )

    def send_count(t):
        return pltpu.make_async_remote_copy(
            src_ref=count_ref, dst_ref=counts.at[c], send_sem=c_send.at[t], recv_sem=c_recv,
            device_id=(s, s * N_Y + t), device_id_type=MESH,
        )

    def send_total(o):
        return pltpu.make_async_remote_copy(
            src_ref=total_ref, dst_ref=total_ref, send_sem=t_send.at[o - 1], recv_sem=t_recv,
            device_id=(lax.rem(s + o, N_GROUP), c), device_id_type=MESH,
        )

    def other(i, yy):
        return lax.rem(z + step_z(i), N_Z) * N_Y + lax.rem(y + yy, N_Y)

    own_kv = pltpu.make_async_copy(kv_ref.at[c], all_ref.at[:, s, rows_of(c), :], self_sem.at[0])
    own_q = pltpu.make_async_copy(q_ref.at[c], qout_ref.at[c], self_sem.at[1])
    own_kv.start()
    for yy in range(1, N_Y):
        send_kv(other(0, yy), 0).start()

    def start_plane(i, carry):
        for yy in range(N_Y):
            send_kv(other(i, yy), i).start()
        return carry

    lax.fori_loop(1, 3, start_plane, 0)
    for t in range(N_Y):
        @pl.when(s * N_Y + t != c)
        def _():
            send_count(t).start()

    lax.fori_loop(3, N_Z, start_plane, 0)
    pack_queries(q_ref, project(2, wq) * SCALE)
    own_q.start()

    def start_q(i, carry):
        for yy in range(N_Y):
            send_q(other(i, yy)).start()
        return carry

    for yy in range(1, N_Y):
        send_q(other(0, yy)).start()
    lax.fori_loop(1, N_Z, start_q, 0)

    def plane(i):
        return lax.rem(z + N_Z - step_z(i), N_Z)

    def hop(slot, i, to, kind, recv, half=None):
        first, size = plane(i) * 128, 128
        if half is not None:
            first, size = first + half * 64, 64
        part = all_ref.at[:, slot, pl.ds(pl.multiple_of(first, 64), size), :]
        return pltpu.make_async_remote_copy(
            src_ref=part, dst_ref=part, send_sem=x_send.at[kind], recv_sem=recv,
            device_id=(to, c), device_id_type=MESH,
        )

    def whole(slot, kind, recv, half=None):
        part = all_ref.at[:, slot, pl.ds(0, ROWS if half is None else ROWS // 2), :]
        return pltpu.make_async_remote_copy(
            src_ref=part, dst_ref=part, send_sem=x_send.at[kind], recv_sem=recv,
            device_id=(partner, c), device_id_type=MESH,
        )

    def send_own(i):
        hop(s, i, right, 0, near_recv.at[0, i]).start()
        hop(s, i, left, 1, near_recv.at[1, i]).start()
        hop(s, i, partner, 2, pair_recv.at[0]).start()

    def send_near(i):
        hop(left, i, left, 0, near_recv.at[0, i]).wait_recv()
        hop(left, i, right, 3, half_recv.at[0, i], half=0).start()
        hop(left, i, partner, 5, pair_recv.at[1]).start()
        hop(right, i, right, 1, near_recv.at[1, i]).wait_recv()
        hop(right, i, left, 4, half_recv.at[1, i], half=1).start()
        hop(right, i, partner, 6, pair_recv.at[2]).start()

    def send_across(i):
        hop(across, i, left, 3, half_recv.at[0, i], half=0).wait_recv()
        hop(across, i, right, 4, half_recv.at[1, i], half=1).wait_recv()
        hop(across, i, partner, 7, pair_recv.at[3]).start()

    def arrive_plane(i):
        part = all_ref.at[:, s, pl.ds(pl.multiple_of(plane(i) * 128, 128), 128), :]
        pltpu.make_async_remote_copy(
            src_ref=part, dst_ref=part, send_sem=kv_send, recv_sem=kv_recv.at[i],
            device_id=(partner, c), device_id_type=MESH,
        ).wait_recv()

    own_kv.wait()
    three = all_ref.at[:, s, pl.ds(pl.multiple_of(z * 128, 128), 96), :]
    pltpu.make_async_remote_copy(
        src_ref=three, dst_ref=three, send_sem=kv_send, recv_sem=kv_recv.at[0],
        device_id=(partner, c), device_id_type=MESH,
    ).wait_recv()
    send_own(0)
    arrive_plane(1)
    send_own(1)
    send_near(0)

    def step(i, carry):
        arrive_plane(i)
        send_own(i)
        send_near(i - 1)
        send_across(i - 2)
        return carry

    lax.fori_loop(2, 5, step, 0)

    @pl.when(owner)
    def _():
        counts[c] = count_ref[...]
        rest = counts.at[pl.ds(0, N_CTX - 1)]
        pltpu.make_async_remote_copy(
            src_ref=rest, dst_ref=rest, send_sem=c_send.at[0], recv_sem=c_recv,
            device_id=(partner, c), device_id_type=MESH,
        ).wait_recv()
        total_ref[...] = jnp.sum(counts[...], axis=0)
        for o in range(1, N_GROUP):
            send_total(o).start()

    lax.fori_loop(5, N_Z, step, 0)
    send_near(N_Z - 1)
    send_across(N_Z - 2)
    send_across(N_Z - 1)

    for t in range(N_Y):
        @pl.when(s * N_Y + t != c)
        def _():
            send_count(t).wait_send()

    @pl.when(owner)
    def _():
        for o in range(1, N_GROUP):
            send_total(o).wait_send()

    @pl.when(jnp.logical_not(owner))
    def _():
        send_total(1).wait_recv()

    own_q.wait()
    rest = pltpu.make_async_remote_copy(
        src_ref=q_ref.at[pl.ds(0, N_CTX - 1)], dst_ref=qout_ref.at[pl.ds(0, N_CTX - 1)],
        send_sem=q_send, recv_sem=q_recv, device_id=(partner, c), device_id_type=MESH,
    )
    rest.wait_recv()
    rest.wait_send()
    sent = kv_ref.at[pl.ds(0, N_CTX - 1)]
    pltpu.make_async_remote_copy(
        src_ref=sent, dst_ref=sent, send_sem=kv_send, recv_sem=kv_recv.at[0],
        device_id=(partner, c), device_id_type=MESH,
    ).wait_send()
    for kind, slot in enumerate((s, s, s, left, right, left, right, across)):
        whole(slot, kind, t_recv, half=0 if kind in (3, 4) else None).wait_send()
    slots = (partner, lax.rem(partner + 6, N_GROUP), lax.rem(partner + 2, N_GROUP), lax.rem(partner + 4, N_GROUP))
    for n, slot in enumerate(slots):
        whole(slot, 2, pair_recv.at[n]).wait_recv()


def spread(packing, series, recon, token, docs, gain, w_query, w_key, w_value):
    anywhere = pl.BlockSpec(memory_space=pltpu.HBM)
    vmem = pl.BlockSpec(memory_space=pltpu.VMEM)
    dma = pltpu.SemaphoreType.DMA
    weight = pltpu.VMEM((D, D), jnp.bfloat16)
    return pl.pallas_call(
        spread_kernel,
        out_shape=(
            jax.ShapeDtypeStruct((PER, N_GROUP, ROWS, 128), jnp.bfloat16),
            jax.ShapeDtypeStruct((N_CTX, QROWS, 128), jnp.bfloat16),
            jax.ShapeDtypeStruct((8, 128), jnp.int32),
        ),
        in_specs=[pl.BlockSpec(memory_space=pltpu.SMEM)] + [vmem] * 5 + [anywhere] * 3,
        out_specs=(anywhere, anywhere, vmem),
        scratch_shapes=[
            pltpu.VMEM((N_CTX, PER, BLK, 128), jnp.bfloat16),
            pltpu.VMEM((N_CTX, QROWS, 128), jnp.bfloat16),
            pltpu.VMEM((8, 128), jnp.int32),
            pltpu.VMEM((N_GROUP, BLK, 128), jnp.float32),
            weight, weight, weight,
            dma((3,)),
            pltpu.VMEM((N_CTX, 8, 128), jnp.int32),
            dma(()), dma((N_Z,)), dma(()), dma(()), dma((N_Y,)), dma(()), dma((2,)),
            dma((8,)), dma((2, N_Z)), dma((2, N_Z)), dma((4,)), dma((N_GROUP - 1,)), dma(()),
        ],
        compiler_params=pltpu.CompilerParams(
            collective_id=0, has_side_effects=True, vmem_limit_bytes=32 << 20
        ),
        name="spread",
    )(packing, series, recon, token, docs, gain, w_query, w_key, w_value)


def attend_kernel(total_ref, q_ref, kv, out_ref, qt, k1, vt, acc, top):
    s = lax.axis_index("group")
    starts = [total_ref[0, d] for d in range(3)]
    first, last = [jnp.int32(0)] + starts, starts + [jnp.int32(N_CTX * 256)]

    def edges(index):
        lo, hi = jnp.full(index.shape, N_CTX * 256), jnp.zeros(index.shape, jnp.int32)
        for d in range(DOCS):
            lo = jnp.where(index == HD + d, first[d], lo)
            hi = jnp.where(index == HD + d, last[d], hi)
        return lo, hi

    col = lax.broadcasted_iota(jnp.int32, (1, ROWS), 1)
    pos = (col // BLK) * 256 + s * BLK + col % BLK
    row = lax.broadcasted_iota(jnp.int32, (HD, 1), 0) + HD
    lo, hi = edges(row)
    own = (pos >= lo) & (pos < hi)
    far = jnp.where(own | (row >= HD + DOCS), 0.0, NEGATIVE)

    a = q_ref[:, 0:BLK, :].reshape(ROWS, 128).astype(jnp.float32).T
    b = q_ref[:, BLK:QROWS, :].astype(jnp.float32)
    b = jnp.concatenate([b, swap(b.reshape(ROWS // 2, 128)).reshape(N_CTX, 16, 128)], axis=1)
    b = b.reshape(ROWS, 128).T
    q_top = []
    for h, part in enumerate((a[0:HD], a[HD:128], b[0:HD])):
        q_top.append(jnp.max(jnp.sum(part * part, axis=0, keepdims=True)))
        qt[h] = jnp.concatenate([part, far], axis=0).astype(jnp.bfloat16)

    r = lax.broadcasted_iota(jnp.int32, (ROWS, 128), 0)
    base = (r // BLK) * 256 + r % BLK
    lo, hi = edges(lax.broadcasted_iota(jnp.int32, (1, 128), 1))
    keys_n = KC * 256
    low = low_half((ROWS, 128))
    vt[:, :, 0:16, :] = jnp.ones((PER, N_CTX // KC, 16, keys_n), jnp.bfloat16)
    small = None
    for h in range(PER):
        for n in range(N_GROUP):
            both = kv[h, n]
            if h == 0:
                own = (base >= lo - n * BLK) & (base < hi - n * BLK)
                mark = jnp.where(own, 1.0, 0.0).astype(jnp.bfloat16)
            else:
                mark = k1[0, n]
            k1[h, n] = jnp.where(low, both, mark)
        norms = jnp.zeros((1, keys_n), jnp.float32)
        for kb in range(N_CTX // KC):
            block = kv[h, :, kb * KC * BLK : (kb + 1) * KC * BLK, :].reshape(keys_n, 128).T
            vt[h, kb, 16:80, :] = block[HD:128]
            keys = block[0:HD].astype(jnp.float32)
            norms = jnp.maximum(norms, jnp.sum(keys * keys, axis=0, keepdims=True))
        fits = q_top[h] * jnp.max(norms) * 1.05 <= BOUND * BOUND
        small = fits if small is None else small & fits

    span = TQ // BLK * 256
    blocks = TQ // BLK

    def tile(t, carry):
        p0 = t * span
        p1 = p0 + span - 1
        lo, hi = jnp.int32(0), jnp.int32(N_CTX * 256)
        for st in starts:
            lo = jnp.maximum(lo, jnp.where(st <= p0, st, 0))
            hi = jnp.minimum(hi, jnp.where(st > p1, st, N_CTX * 256))
        begin, end = lo // keys_n, (hi + keys_n - 1) // keys_n
        cols = pl.ds(pl.multiple_of(t * TQ, TQ), TQ)

        def scores(h, kb):
            rows = pl.ds(pl.multiple_of(kb * KC * BLK, KC * BLK), KC * BLK)
            keys = k1[h, :, rows, :].reshape(keys_n, 128)
            return jnp.dot(keys, qt[h, :, cols], preferred_element_type=jnp.float32)

        def summed(h, kb, p):
            return jnp.dot(vt[h, kb], p, preferred_element_type=jnp.float32)

        acc[...] = jnp.zeros_like(acc)

        @pl.when(small)
        def _():
            def body(kb, carry):
                weights = [scores(h, kb) for h in range(PER)]
                weights = [jnp.exp2(w).astype(jnp.bfloat16) for w in weights]
                sums = [summed(h, kb, weights[h]) for h in range(PER)]
                for h in range(PER):
                    acc[h] += sums[h]
                return carry

            lax.fori_loop(begin, end, body, 0)

        @pl.when(jnp.logical_not(small))
        def _():
            top[...] = jnp.full_like(top, NEGATIVE)

            def body(kb, carry):
                all_scores = [scores(h, kb) for h in range(PER)]
                for h, sc in enumerate(all_scores):
                    old = top[h]
                    new = jnp.maximum(old, jnp.max(sc, axis=0, keepdims=True))
                    top[h] = new
                    weights = jnp.exp2(sc - new).astype(jnp.bfloat16)
                    acc[h] = acc[h] * jnp.exp2(old - new) + summed(h, kb, weights)
                return carry

            lax.fori_loop(begin, end, body, 0)

        def attended(h):
            return acc[h, 16:80, :] / acc[h, 0:1, :]

        here = pl.ds(t * blocks, blocks)
        o = jnp.concatenate([attended(0), attended(1)], axis=0).T
        out_ref[here, 0:BLK] = o.astype(jnp.bfloat16).reshape(blocks, BLK, 128)
        o = attended(2)
        o = jnp.concatenate([o, o], axis=0).T.reshape(blocks, BLK, 128)
        one, two = o[:, 0:16].reshape(TQ // 2, 128), o[:, 16:32].reshape(TQ // 2, 128)
        out_ref[here, BLK:QROWS] = join(one, two).astype(jnp.bfloat16).reshape(blocks, 16, 128)
        return carry

    lax.fori_loop(0, ROWS // TQ, tile, 0)


def attend(total, q, kv):
    vmem = pl.BlockSpec(memory_space=pltpu.VMEM)
    wide = pltpu.VMEM((PER, N_GROUP, ROWS, 128), jnp.bfloat16)
    return pl.pallas_call(
        attend_kernel,
        out_shape=jax.ShapeDtypeStruct((N_CTX, QROWS, 128), jnp.bfloat16),
        in_specs=[pl.BlockSpec(memory_space=pltpu.SMEM), vmem, vmem],
        out_specs=vmem,
        scratch_shapes=[
            pltpu.VMEM((PER, 128, ROWS), jnp.bfloat16),
            wide,
            pltpu.VMEM((PER, N_CTX // KC, 80, KC * 256), jnp.bfloat16),
            pltpu.VMEM((PER, 80, TQ), jnp.float32),
            pltpu.VMEM((PER, 1, TQ), jnp.float32),
        ],
        compiler_params=pltpu.CompilerParams(vmem_limit_bytes=40 << 20),
        name="attend",
    )(total, q, kv)


def finish_kernel(packing_ref, att_ref, series_ref, recon_ref, token_ref, w_ref, out_ref, lhs, w2):
    order = [PER * t + n for t in range(TRIPLES) for n in range(2)] + [2, 5, 8, 11]
    for n, head in enumerate(order):
        w2[n * HD : (n + 1) * HD, :] = w_ref[head * HD : (head + 1) * HD, :]
    for k in range(N_GROUP):
        g = packing_ref[k]
        rows = slice(k * BLK, (k + 1) * BLK)
        for t in range(TRIPLES):
            lhs[rows, t * 128 : (t + 1) * 128] = att_ref[g * TRIPLES + t, 0:BLK]
        for n in range(2):
            a = att_ref[g * TRIPLES + 2 * n, BLK:QROWS].astype(jnp.float32)
            b = att_ref[g * TRIPLES + 2 * n + 1, BLK:QROWS].astype(jnp.float32)
            cols = slice((TRIPLES + n) * 128, (TRIPLES + n + 1) * 128)
            lhs[k * BLK : k * BLK + 16, cols] = join(a, swap(b)).astype(jnp.bfloat16)
            lhs[k * BLK + 16 : (k + 1) * BLK, cols] = join(swap(a), b).astype(jnp.bfloat16)
    mixed = jnp.dot(lhs[...], w2[...], preferred_element_type=jnp.float32)
    rows = masked_rows(series_ref[...], row_mask(recon_ref), token_ref)
    out_ref[...] = (rows + mixed).astype(jnp.bfloat16)


def finish(packing, att, series, recon, token, w_out):
    vmem = pl.BlockSpec(memory_space=pltpu.VMEM)
    return pl.pallas_call(
        finish_kernel,
        out_shape=jax.ShapeDtypeStruct(series.shape, jnp.bfloat16),
        in_specs=[pl.BlockSpec(memory_space=pltpu.SMEM)] + [vmem] * 5,
        out_specs=vmem,
        scratch_shapes=[pltpu.VMEM((N_GROUP * BLK, D), jnp.bfloat16), pltpu.VMEM((D, D), jnp.bfloat16)],
        compiler_params=pltpu.CompilerParams(vmem_limit_bytes=48 << 20),
        name="finish",
    )(packing, att, series, recon, token, w_out)


def on_device(
    series, recon_mask, mask_token, packing_list, doc_ids, norm_gain, w_query, w_key, w_value, w_out
):
    recon = recon_mask.reshape(1, -1)
    token = mask_token.reshape(1, -1)
    all_kv, q_rows, total = spread(
        packing_list, series.reshape(N_GROUP, BLK, D), recon, token, doc_ids, norm_gain.reshape(1, -1),
        *(pltpu.with_memory_space_constraint(w, pltpu.HBM) for w in (w_query, w_key, w_value)),
    )
    att = attend(total, q_rows, all_kv)
    back = lax.all_to_all(att, "ctx", split_axis=0, concat_axis=0, tiled=True)
    return finish(packing_list, back, series, recon, token, w_out)


def solution(mesh):
    split = P(("group", "ctx"))
    in_specs = (
        P(("group", "ctx"), None), split, P(), split, P("group", "ctx"), P(), P(), P(), P(), P(),
    )
    return jax.shard_map(
        on_device, mesh=mesh, in_specs=in_specs, out_specs=P(("group", "ctx"), None), check_vma=False
    )
```

```python
import functools
import math

import jax
import jax.numpy as jnp
from jax import lax
from jax.experimental import pallas as pl
from jax.experimental.pallas import tpu as pltpu
from jax.sharding import PartitionSpec as P

D = 768
HEADS = 12
HD = 64
BLK = 32
N_GROUP = 8
N_CTX = 32
N_Z = 8
N_Y = 4
TRIPLES = 4
PER = 3
QROWS = 48
ROWS = N_CTX * BLK
NEGATIVE = -1e30
DOCS = 4
BOUND = 100.0
SCALE = math.log2(math.e) / math.sqrt(HD)
TQ = 256
KC = 4
MESH = pl.DeviceIdType.MESH


def low_half(shape):
    return lax.broadcasted_iota(jnp.int32, shape, len(shape) - 1) < HD


def swap(x):
    return pltpu.roll(x, HD, 1)


def join(a, b):
    return jnp.where(low_half(a.shape), a, b)


def row_mask(recon_ref):
    flags = recon_ref[...].astype(jnp.float32)
    return jnp.broadcast_to(flags, (128, flags.shape[1])).T


def masked_rows(rows, flags, token_ref):
    flags = jnp.concatenate([flags] * (D // 128), axis=1)
    token = token_ref[...].astype(jnp.float32).reshape(1, D)
    return jnp.where(flags == 1.0, token, rows.astype(jnp.float32))


def normed_rows(packing_ref, series_ref, recon_ref, token_ref, gain_ref, flags):
    flags[...] = row_mask(recon_ref).reshape(N_GROUP, BLK, 128)
    pieces = []
    for g in range(N_GROUP):
        at = jnp.int32(0)
        for k in range(1, N_GROUP):
            at = jnp.where(packing_ref[k] == g, k, at)
        pieces.append(masked_rows(series_ref[at], flags[at], token_ref))
    x = jnp.concatenate(pieces, axis=0)
    factor = lax.rsqrt(jnp.mean(x * x, axis=-1, keepdims=True) + 1e-06)
    return (x * factor * gain_ref[...].astype(jnp.float32).reshape(1, D)).astype(jnp.bfloat16)


def document_counts(doc_ref):
    ids = doc_ref[...]
    lane = lax.broadcasted_iota(jnp.int32, (8, 128), 1)
    count = jnp.zeros((8, 128), jnp.int32)
    for d in range(DOCS - 1):
        below = jnp.sum((ids <= d).astype(jnp.float32), axis=1, keepdims=True).astype(jnp.int32)
        count = jnp.where(lane == d, below, count)
    return count


def piece(values, g):
    return values[g * BLK : (g + 1) * BLK]


def pack_keys(kv_ref, key, value):
    for m in range(HEADS // 2):
        kp, vp = key[:, m * 128 : (m + 1) * 128], value[:, m * 128 : (m + 1) * 128]
        for head, kv in ((2 * m, join(kp, swap(vp))), (2 * m + 1, join(swap(kp), vp))):
            kv = kv.astype(jnp.bfloat16)
            for g in range(N_GROUP):
                kv_ref[g * TRIPLES + head // PER, head % PER] = piece(kv, g)


def pack_queries(q_ref, query):
    for t in range(TRIPLES):
        pair = [query[:, m * 128 : (m + 1) * 128] for m in (3 * t // 2, 3 * t // 2 + 1)]
        if t % 2 == 0:
            first, last = pair[0], pair[1]
        else:
            first, last = join(swap(pair[0]), swap(pair[1])), swap(pair[1])
        first = first.astype(jnp.bfloat16)
        swapped = swap(last)
        for g in range(N_GROUP):
            to = g * TRIPLES + t
            q_ref[to, 0:BLK] = piece(first, g)
            half = join(last[g * BLK : g * BLK + 16], swapped[g * BLK + 16 : (g + 1) * BLK])
            q_ref[to, BLK:QROWS] = half.astype(jnp.bfloat16)


def step_z(i):
    return lax.rem(N_Z + (1 - 2 * lax.rem(i + 1, 2)) * ((i + 1) // 2), N_Z)


def spread_kernel(
    packing_hbm, token_hbm, gain_hbm, series_hbm, recon_hbm, doc_hbm, wq_ref, wk_ref, wv_ref,
    k1_ref, vt_ref, qout_ref, total_ref, norm_ref,
    packing_ref, token_ref, gain_ref, series_ref, recon_ref, doc_ref, all_ref, norms, kv_ref, q_ref, count_ref, flags, wq, wk, wv, w_sem, counts, kv_send, kv_recv, q_send, q_recv, c_send, c_recv, self_sem,
    x_send, near_recv, half_recv, pair_recv, t_send, t_recv,
):
    s = lax.axis_index("group")
    c = lax.axis_index("ctx")
    z, y = c // N_Y, lax.rem(c, N_Y)
    partner = s + 1 - 2 * lax.rem(s, 2)
    right, left, across = lax.rem(s + 2, N_GROUP), lax.rem(s + 6, N_GROUP), lax.rem(s + 4, N_GROUP)
    owner = z == s
    loads = [
        pltpu.make_async_copy(src, dst, w_sem.at[n])
        for n, (src, dst) in enumerate((
            (wk_ref, wk), (wv_ref, wv), (wq_ref, wq),
            (series_hbm, series_ref), (recon_hbm, recon_ref), (doc_hbm, doc_ref),
            (packing_hbm, packing_ref), (token_hbm, token_ref), (gain_hbm, gain_ref),
        ))
    ]
    for n in (3, 4, 5, 6, 7, 8, 0, 1, 2):
        loads[n].start()
    bar = pltpu.get_barrier_semaphore()

    def greet(o, carry):
        pl.semaphore_signal(bar, inc=1, device_id=(s, lax.rem(c + o, N_CTX)), device_id_type=MESH)
        return carry

    lax.fori_loop(1, N_CTX, greet, 0)
    for o in range(1, N_GROUP):
        pl.semaphore_signal(bar, inc=1, device_id=(lax.rem(s + o, N_GROUP), c), device_id_type=MESH)
    vt_ref[:, :, 0:16, :] = jnp.ones((PER, N_Z, 16, ROWS), jnp.bfloat16)
    norms[...] = jnp.zeros_like(norms)
    for n in range(3, 9):
        loads[n].wait()
    count_ref[...] = document_counts(doc_ref)
    normed = normed_rows(packing_ref, series_ref, recon_ref, token_ref, gain_ref, flags)

    def project(n, w):
        loads[n].wait()
        return jnp.dot(normed, w[...], preferred_element_type=jnp.float32)

    pack_keys(kv_ref, project(0, wk), project(1, wv))
    pl.semaphore_wait(bar, N_CTX - 1 + N_GROUP - 1)

    def rows_of(d):
        return pl.ds(pl.multiple_of(d * BLK, BLK), BLK)

    def send_kv(d, i):
        return pltpu.make_async_remote_copy(
            src_ref=kv_ref.at[d], dst_ref=all_ref.at[:, s, rows_of(c), :],
            send_sem=kv_send, recv_sem=kv_recv.at[i],
            device_id=(s, d), device_id_type=MESH,
        )

    def send_q(d):
        return pltpu.make_async_remote_copy(
            src_ref=q_ref.at[d], dst_ref=qout_ref.at[c], send_sem=q_send, recv_sem=q_recv,
            device_id=(s, d), device_id_type=MESH,
        )

    def send_count(t):
        return pltpu.make_async_remote_copy(
            src_ref=count_ref, dst_ref=counts.at[c], send_sem=c_send.at[t], recv_sem=c_recv,
            device_id=(s, s * N_Y + t), device_id_type=MESH,
        )

    def send_total(o):
        return pltpu.make_async_remote_copy(
            src_ref=total_ref, dst_ref=total_ref, send_sem=t_send.at[o - 1], recv_sem=t_recv,
            device_id=(lax.rem(s + o, N_GROUP), c), device_id_type=MESH,
        )

    def other(i, yy):
        return lax.rem(z + step_z(i), N_Z) * N_Y + lax.rem(y + yy, N_Y)

    own_kv = pltpu.make_async_copy(kv_ref.at[c], all_ref.at[:, s, rows_of(c), :], self_sem.at[0])
    own_q = pltpu.make_async_copy(q_ref.at[c], qout_ref.at[c], self_sem.at[1])
    own_kv.start()
    for t in range(N_Y):
        @pl.when(s * N_Y + t != c)
        def _():
            send_count(t).start()

    for yy in range(1, N_Y):
        send_kv(other(0, yy), 0).start()

    def start_plane(i, carry):
        for yy in range(N_Y):
            send_kv(other(i, yy), i).start()
        return carry

    lax.fori_loop(1, N_Z, start_plane, 0)
    pack_queries(q_ref, project(2, wq) * SCALE)
    own_q.start()

    def start_q(i, carry):
        for yy in range(N_Y):
            send_q(other(i, yy)).start()
        return carry


    def plane(i):
        return lax.rem(z + N_Z - step_z(i), N_Z)

    def hop(slot, i, to, kind, recv, half=None):
        first, size = plane(i) * 128, 128
        if half is not None:
            first, size = first + half * 64, 64
        part = all_ref.at[:, slot, pl.ds(pl.multiple_of(first, 64), size), :]
        return pltpu.make_async_remote_copy(
            src_ref=part, dst_ref=part, send_sem=x_send.at[kind], recv_sem=recv,
            device_id=(to, c), device_id_type=MESH,
        )

    def whole(slot, kind, recv, half=None):
        part = all_ref.at[:, slot, pl.ds(0, ROWS if half is None else ROWS // 2), :]
        return pltpu.make_async_remote_copy(
            src_ref=part, dst_ref=part, send_sem=x_send.at[kind], recv_sem=recv,
            device_id=(partner, c), device_id_type=MESH,
        )

    def send_own(i):
        hop(s, i, right, 0, near_recv.at[0, i]).start()
        hop(s, i, left, 1, near_recv.at[1, i]).start()
        hop(s, i, partner, 2, pair_recv.at[0, i]).start()

    def send_near(i):
        hop(left, i, left, 0, near_recv.at[0, i]).wait_recv()
        hop(left, i, right, 3, half_recv.at[0, i], half=0).start()
        hop(left, i, partner, 5, pair_recv.at[1, i]).start()
        hop(right, i, right, 1, near_recv.at[1, i]).wait_recv()
        hop(right, i, left, 4, half_recv.at[1, i], half=1).start()
        hop(right, i, partner, 6, pair_recv.at[2, i]).start()

    def send_across(i):
        hop(across, i, left, 3, half_recv.at[0, i], half=0).wait_recv()
        hop(across, i, right, 4, half_recv.at[1, i], half=1).wait_recv()
        hop(across, i, partner, 7, pair_recv.at[3, i]).start()

    slots = (partner, lax.rem(partner + 6, N_GROUP), lax.rem(partner + 2, N_GROUP), lax.rem(partner + 4, N_GROUP))
    r = lax.broadcasted_iota(jnp.int32, (128, 128), 0)
    base = ((r // BLK) * 256 + r % BLK).astype(jnp.float32)
    lane = lax.broadcasted_iota(jnp.int32, (1, 128), 1)
    low = low_half((128, 128))

    def lay_out(i):
        for n, slot in enumerate(slots):
            hop(slot, i, partner, 2, pair_recv.at[n, i]).wait_recv()
        at = plane(i)
        rows = pl.ds(pl.multiple_of(at * 128, 128), 128)
        totals = total_ref[...].astype(jnp.float32)
        lo = pltpu.roll(totals, HD + 1, 1)[0:1]
        hi = jnp.where(lane == HD + DOCS - 1, float(N_CTX * 256), pltpu.roll(totals, HD, 1)[0:1])
        first = (at * 1024).astype(jnp.float32)
        lo, hi = lo - first, hi - first
        for n in range(N_GROUP):
            own = (base >= lo - n * BLK) & (base < hi - n * BLK)
            mark = jnp.where(own, 1.0, 0.0).astype(jnp.bfloat16)
            for h in range(PER):
                k1_ref[h, n, rows, :] = jnp.where(low, all_ref[h, n, rows, :], mark)
        for h in range(PER):
            block = all_ref[h, :, rows, :].reshape(ROWS, 128).T
            vt_ref[h, at, 16:80, :] = block[HD:128]
            keys = block[0:HD].astype(jnp.float32)
            norms[h] = jnp.maximum(norms[h], jnp.sum(keys * keys, axis=0, keepdims=True))

    def arrive_plane(i):
        part = all_ref.at[:, s, pl.ds(pl.multiple_of(plane(i) * 128, 128), 128), :]
        pltpu.make_async_remote_copy(
            src_ref=part, dst_ref=part, send_sem=kv_send, recv_sem=kv_recv.at[i],
            device_id=(partner, c), device_id_type=MESH,
        ).wait_recv()

    own_kv.wait()
    three = all_ref.at[:, s, pl.ds(pl.multiple_of(z * 128, 128), 96), :]
    pltpu.make_async_remote_copy(
        src_ref=three, dst_ref=three, send_sem=kv_send, recv_sem=kv_recv.at[0],
        device_id=(partner, c), device_id_type=MESH,
    ).wait_recv()
    send_own(0)
    arrive_plane(1)
    send_own(1)
    send_near(0)
    for yy in range(1, N_Y):
        send_q(other(0, yy)).start()
    lax.fori_loop(1, N_Z, start_q, 0)
    arrive_plane(2)
    send_own(2)
    send_near(1)
    send_across(0)

    def step(i, carry):
        arrive_plane(i)
        send_own(i)
        send_near(i - 1)
        send_across(i - 2)
        lay_out(i - 3)
        return carry

    @pl.when(owner)
    def _():
        counts[c] = count_ref[...]
        rest = counts.at[pl.ds(0, N_CTX - 1)]
        pltpu.make_async_remote_copy(
            src_ref=rest, dst_ref=rest, send_sem=c_send.at[0], recv_sem=c_recv,
            device_id=(partner, c), device_id_type=MESH,
        ).wait_recv()
        total_ref[...] = jnp.sum(counts[...], axis=0)
        for o in range(1, N_GROUP):
            send_total(o).start()

    @pl.when(jnp.logical_not(owner))
    def _():
        send_total(1).wait_recv()

    lax.fori_loop(3, N_Z, step, 0)
    send_near(N_Z - 1)
    send_across(N_Z - 2)
    lay_out(N_Z - 3)
    send_across(N_Z - 1)
    lay_out(N_Z - 2)
    lay_out(N_Z - 1)
    sub = lax.broadcasted_iota(jnp.int32, (8, 128), 0)
    top = jnp.zeros((8, 128), jnp.float32)
    for h in range(PER):
        top = jnp.where(sub == h, jnp.max(norms[h], axis=1, keepdims=True), top)
    norm_ref[...] = top

    for t in range(N_Y):
        @pl.when(s * N_Y + t != c)
        def _():
            send_count(t).wait_send()

    @pl.when(owner)
    def _():
        for o in range(1, N_GROUP):
            send_total(o).wait_send()

    own_q.wait()
    rest = pltpu.make_async_remote_copy(
        src_ref=q_ref.at[pl.ds(0, N_CTX - 1)], dst_ref=qout_ref.at[pl.ds(0, N_CTX - 1)],
        send_sem=q_send, recv_sem=q_recv, device_id=(partner, c), device_id_type=MESH,
    )
    rest.wait_recv()
    rest.wait_send()
    sent = kv_ref.at[pl.ds(0, N_CTX - 1)]
    pltpu.make_async_remote_copy(
        src_ref=sent, dst_ref=sent, send_sem=kv_send, recv_sem=kv_recv.at[0],
        device_id=(partner, c), device_id_type=MESH,
    ).wait_send()
    for kind, slot in enumerate((s, s, s, left, right, left, right, across)):
        whole(slot, kind, t_recv, half=0 if kind in (3, 4) else None).wait_send()


def hbm(x):
    return pltpu.with_memory_space_constraint(x, pltpu.HBM)


def spread(packing, series, recon, token, docs, gain, w_query, w_key, w_value):
    anywhere = pl.BlockSpec(memory_space=pltpu.HBM)
    vmem = pl.BlockSpec(memory_space=pltpu.VMEM)
    dma = pltpu.SemaphoreType.DMA
    weight = pltpu.VMEM((D, D), jnp.bfloat16)
    return pl.pallas_call(
        spread_kernel,
        out_shape=(
            jax.ShapeDtypeStruct((PER, N_GROUP, ROWS, 128), jnp.bfloat16),
            jax.ShapeDtypeStruct((PER, N_Z, 80, ROWS), jnp.bfloat16),
            jax.ShapeDtypeStruct((N_CTX, QROWS, 128), jnp.bfloat16),
            jax.ShapeDtypeStruct((8, 128), jnp.int32),
            jax.ShapeDtypeStruct((8, 128), jnp.float32),
        ),
        in_specs=[anywhere] * 9,
        out_specs=(vmem, vmem, anywhere, vmem, vmem),
        scratch_shapes=[
            pltpu.SMEM((N_GROUP,), jnp.int32),
            pltpu.VMEM((D,), jnp.bfloat16),
            pltpu.VMEM((D,), jnp.bfloat16),
            pltpu.VMEM((N_GROUP, BLK, D), jnp.bfloat16),
            pltpu.VMEM((1, N_GROUP * BLK), jnp.int32),
            pltpu.VMEM((1, N_GROUP * BLK), jnp.int32),
            pltpu.VMEM((PER, N_GROUP, ROWS, 128), jnp.bfloat16),
            pltpu.VMEM((PER, 1, ROWS), jnp.float32),
            pltpu.VMEM((N_CTX, PER, BLK, 128), jnp.bfloat16),
            pltpu.VMEM((N_CTX, QROWS, 128), jnp.bfloat16),
            pltpu.VMEM((8, 128), jnp.int32),
            pltpu.VMEM((N_GROUP, BLK, 128), jnp.float32),
            weight, weight, weight,
            dma((9,)),
            pltpu.VMEM((N_CTX, 8, 128), jnp.int32),
            dma(()), dma((N_Z,)), dma(()), dma(()), dma((N_Y,)), dma(()), dma((2,)),
            dma((8,)), dma((2, N_Z)), dma((2, N_Z)), dma((4, N_Z)), dma((N_GROUP - 1,)), dma(()),
        ],
        compiler_params=pltpu.CompilerParams(
            collective_id=0, has_side_effects=True, vmem_limit_bytes=32 << 20
        ),
        name="spread",
    )(*(hbm(x) for x in (packing, token, gain, series, recon, docs, w_query, w_key, w_value)))


def attend_kernel(total_ref, norm_ref, q_ref, k1, vt, out_ref, qt, acc, top):
    s = lax.axis_index("group")
    starts = [total_ref[0, d] for d in range(3)]
    first, last = [jnp.int32(0)] + starts, starts + [jnp.int32(N_CTX * 256)]

    def edges(index):
        lo, hi = jnp.full(index.shape, N_CTX * 256), jnp.zeros(index.shape, jnp.int32)
        for d in range(DOCS):
            lo = jnp.where(index == HD + d, first[d], lo)
            hi = jnp.where(index == HD + d, last[d], hi)
        return lo, hi

    col = lax.broadcasted_iota(jnp.int32, (1, ROWS), 1)
    pos = (col // BLK) * 256 + s * BLK + col % BLK
    row = lax.broadcasted_iota(jnp.int32, (HD, 1), 0) + HD
    lo, hi = edges(row)
    own = (pos >= lo) & (pos < hi)
    far = jnp.where(own | (row >= HD + DOCS), 0.0, NEGATIVE)

    a = q_ref[:, 0:BLK, :].reshape(ROWS, 128).astype(jnp.float32).T
    b = q_ref[:, BLK:QROWS, :].astype(jnp.float32)
    b = jnp.concatenate([b, swap(b.reshape(ROWS // 2, 128)).reshape(N_CTX, 16, 128)], axis=1)
    b = b.reshape(ROWS, 128).T
    q_top = []
    for h, part in enumerate((a[0:HD], a[HD:128], b[0:HD])):
        q_top.append(jnp.max(jnp.sum(part * part, axis=0, keepdims=True)))
        qt[h] = jnp.concatenate([part, far], axis=0).astype(jnp.bfloat16)

    keys_n = KC * 256
    small = None
    for h in range(PER):
        fits = q_top[h] * norm_ref[h, 0] * 1.05 <= BOUND * BOUND
        small = fits if small is None else small & fits

    span = TQ // BLK * 256
    blocks = TQ // BLK

    def tile(t, carry):
        p0 = t * span
        p1 = p0 + span - 1
        lo, hi = jnp.int32(0), jnp.int32(N_CTX * 256)
        for st in starts:
            lo = jnp.maximum(lo, jnp.where(st <= p0, st, 0))
            hi = jnp.minimum(hi, jnp.where(st > p1, st, N_CTX * 256))
        begin, end = lo // keys_n, (hi + keys_n - 1) // keys_n
        cols = pl.ds(pl.multiple_of(t * TQ, TQ), TQ)

        def scores(h, kb):
            rows = pl.ds(pl.multiple_of(kb * KC * BLK, KC * BLK), KC * BLK)
            keys = k1[h, :, rows, :].reshape(keys_n, 128)
            return jnp.dot(keys, qt[h, :, cols], preferred_element_type=jnp.float32)

        def summed(h, kb, p):
            return jnp.dot(vt[h, kb], p, preferred_element_type=jnp.float32)

        acc[...] = jnp.zeros_like(acc)

        @pl.when(small)
        def _():
            def body(kb, carry):
                weights = [scores(h, kb) for h in range(PER)]
                weights = [jnp.exp2(w).astype(jnp.bfloat16) for w in weights]
                sums = [summed(h, kb, weights[h]) for h in range(PER)]
                for h in range(PER):
                    acc[h] += sums[h]
                return carry

            lax.fori_loop(begin, end, body, 0)

        @pl.when(jnp.logical_not(small))
        def _():
            top[...] = jnp.full_like(top, NEGATIVE)

            def body(kb, carry):
                all_scores = [scores(h, kb) for h in range(PER)]
                for h, sc in enumerate(all_scores):
                    old = top[h]
                    new = jnp.maximum(old, jnp.max(sc, axis=0, keepdims=True))
                    top[h] = new
                    weights = jnp.exp2(sc - new).astype(jnp.bfloat16)
                    acc[h] = acc[h] * jnp.exp2(old - new) + summed(h, kb, weights)
                return carry

            lax.fori_loop(begin, end, body, 0)

        def attended(h):
            return acc[h, 16:80, :] / acc[h, 0:1, :]

        here = pl.ds(t * blocks, blocks)
        o = jnp.concatenate([attended(0), attended(1)], axis=0).T
        out_ref[here, 0:BLK] = o.astype(jnp.bfloat16).reshape(blocks, BLK, 128)
        o = attended(2)
        o = jnp.concatenate([o, o], axis=0).T.reshape(blocks, BLK, 128)
        one, two = o[:, 0:16].reshape(TQ // 2, 128), o[:, 16:32].reshape(TQ // 2, 128)
        out_ref[here, BLK:QROWS] = join(one, two).astype(jnp.bfloat16).reshape(blocks, 16, 128)
        return carry

    lax.fori_loop(0, ROWS // TQ, tile, 0)


def attend(total, norms, q, k1, vt):
    vmem = pl.BlockSpec(memory_space=pltpu.VMEM)
    smem = pl.BlockSpec(memory_space=pltpu.SMEM)
    return pl.pallas_call(
        attend_kernel,
        out_shape=jax.ShapeDtypeStruct((N_CTX, QROWS, 128), jnp.bfloat16),
        in_specs=[smem, smem, vmem, vmem, vmem],
        out_specs=vmem,
        scratch_shapes=[
            pltpu.VMEM((PER, 128, ROWS), jnp.bfloat16),
            pltpu.VMEM((PER, 80, TQ), jnp.float32),
            pltpu.VMEM((PER, 1, TQ), jnp.float32),
        ],
        compiler_params=pltpu.CompilerParams(vmem_limit_bytes=32 << 20),
        name="attend",
    )(total, norms, q, k1, vt)


def finish_kernel(packing_ref, att_ref, series_ref, recon_ref, token_ref, w_ref, out_ref, lhs, w2):
    order = [PER * t + n for t in range(TRIPLES) for n in range(2)] + [2, 5, 8, 11]
    for n, head in enumerate(order):
        w2[n * HD : (n + 1) * HD, :] = w_ref[head * HD : (head + 1) * HD, :]
    for k in range(N_GROUP):
        g = packing_ref[k]
        rows = slice(k * BLK, (k + 1) * BLK)
        for t in range(TRIPLES):
            lhs[rows, t * 128 : (t + 1) * 128] = att_ref[g * TRIPLES + t, 0:BLK]
        for n in range(2):
            a = att_ref[g * TRIPLES + 2 * n, BLK:QROWS].astype(jnp.float32)
            b = att_ref[g * TRIPLES + 2 * n + 1, BLK:QROWS].astype(jnp.float32)
            cols = slice((TRIPLES + n) * 128, (TRIPLES + n + 1) * 128)
            lhs[k * BLK : k * BLK + 16, cols] = join(a, swap(b)).astype(jnp.bfloat16)
            lhs[k * BLK + 16 : (k + 1) * BLK, cols] = join(swap(a), b).astype(jnp.bfloat16)
    mixed = jnp.dot(lhs[...], w2[...], preferred_element_type=jnp.float32)
    rows = masked_rows(series_ref[...], row_mask(recon_ref), token_ref)
    out_ref[...] = (rows + mixed).astype(jnp.bfloat16)


def finish(packing, att, series, recon, token, w_out):
    vmem = pl.BlockSpec(memory_space=pltpu.VMEM)
    return pl.pallas_call(
        finish_kernel,
        out_shape=jax.ShapeDtypeStruct(series.shape, jnp.bfloat16),
        in_specs=[pl.BlockSpec(memory_space=pltpu.SMEM)] + [vmem] * 5,
        out_specs=vmem,
        scratch_shapes=[pltpu.VMEM((N_GROUP * BLK, D), jnp.bfloat16), pltpu.VMEM((D, D), jnp.bfloat16)],
        compiler_params=pltpu.CompilerParams(vmem_limit_bytes=48 << 20),
        name="finish",
    )(packing, att, series, recon, token, w_out)


def on_device(
    series, recon_mask, mask_token, packing_list, doc_ids, norm_gain, w_query, w_key, w_value, w_out
):
    recon = recon_mask.reshape(1, -1)
    token = mask_token
    k1, vt, q_rows, total, norms = spread(
        packing_list, series.reshape(N_GROUP, BLK, D), recon, token, doc_ids, norm_gain,
        w_query, w_key, w_value,
    )
    att = attend(total, norms, q_rows, k1, vt)
    back = lax.all_to_all(att, "ctx", split_axis=0, concat_axis=0, tiled=True)
    return finish(packing_list, back, series, recon, token, w_out)


def solution(mesh):
    split = P(("group", "ctx"))
    in_specs = (
        P(("group", "ctx"), None), split, P(), split, P("group", "ctx"), P(), P(), P(), P(), P(),
    )
    return jax.shard_map(
        on_device, mesh=mesh, in_specs=in_specs, out_specs=P(("group", "ctx"), None), check_vma=False
    )
```

```python
import functools
import math

import jax
import jax.numpy as jnp
from jax import lax
from jax.experimental import pallas as pl
from jax.experimental.pallas import tpu as pltpu
from jax.sharding import PartitionSpec as P

D = 768
HEADS = 12
HD = 64
BLK = 32
N_GROUP = 8
N_CTX = 32
N_Z = 8
N_Y = 4
TRIPLES = 4
PER = 3
QROWS = 48
ROWS = N_CTX * BLK
NEGATIVE = -1e30
DOCS = 4
BOUND = 100.0
SCALE = math.log2(math.e) / math.sqrt(HD)
TQ = 256
KC = 4
MESH = pl.DeviceIdType.MESH


def low_half(shape):
    return lax.broadcasted_iota(jnp.int32, shape, len(shape) - 1) < HD


def swap(x):
    return pltpu.roll(x, HD, 1)


def join(a, b):
    return jnp.where(low_half(a.shape), a, b)


def row_mask(recon_ref):
    flags = recon_ref[...].astype(jnp.float32)
    return jnp.broadcast_to(flags, (128, flags.shape[1])).T


def masked_rows(rows, flags, token_ref):
    flags = jnp.concatenate([flags] * (D // 128), axis=1)
    token = token_ref[...].astype(jnp.float32).reshape(1, D)
    return jnp.where(flags == 1.0, token, rows.astype(jnp.float32))


def normed_rows(packing_ref, series_ref, recon_ref, token_ref, gain_ref, flags):
    flags[...] = row_mask(recon_ref).reshape(N_GROUP, BLK, 128)
    pieces = []
    for g in range(N_GROUP):
        at = jnp.int32(0)
        for k in range(1, N_GROUP):
            at = jnp.where(packing_ref[k] == g, k, at)
        pieces.append(masked_rows(series_ref[at], flags[at], token_ref))
    x = jnp.concatenate(pieces, axis=0)
    factor = lax.rsqrt(jnp.mean(x * x, axis=-1, keepdims=True) + 1e-06)
    return (x * factor * gain_ref[...].astype(jnp.float32).reshape(1, D)).astype(jnp.bfloat16)


def document_counts(doc_ref):
    ids = doc_ref[...]
    lane = lax.broadcasted_iota(jnp.int32, (8, 128), 1)
    count = jnp.zeros((8, 128), jnp.int32)
    for d in range(DOCS - 1):
        below = jnp.sum((ids <= d).astype(jnp.float32), axis=1, keepdims=True).astype(jnp.int32)
        count = jnp.where(lane == d, below, count)
    return count


def piece(values, g):
    return values[g * BLK : (g + 1) * BLK]


def pack_keys(kv_ref, key, value):
    for m in range(HEADS // 2):
        kp, vp = key[:, m * 128 : (m + 1) * 128], value[:, m * 128 : (m + 1) * 128]
        for head, kv in ((2 * m, join(kp, swap(vp))), (2 * m + 1, join(swap(kp), vp))):
            kv = kv.astype(jnp.bfloat16)
            for g in range(N_GROUP):
                kv_ref[g * TRIPLES + head // PER, head % PER] = piece(kv, g)


def pack_queries(q_ref, query):
    for t in range(TRIPLES):
        pair = [query[:, m * 128 : (m + 1) * 128] for m in (3 * t // 2, 3 * t // 2 + 1)]
        if t % 2 == 0:
            first, last = pair[0], pair[1]
        else:
            first, last = join(swap(pair[0]), swap(pair[1])), swap(pair[1])
        first = first.astype(jnp.bfloat16)
        swapped = swap(last)
        for g in range(N_GROUP):
            to = g * TRIPLES + t
            q_ref[to, 0:BLK] = piece(first, g)
            half = join(last[g * BLK : g * BLK + 16], swapped[g * BLK + 16 : (g + 1) * BLK])
            q_ref[to, BLK:QROWS] = half.astype(jnp.bfloat16)


def step_z(i):
    return lax.rem(N_Z + (1 - 2 * lax.rem(i + 1, 2)) * ((i + 1) // 2), N_Z)


def spread_kernel(
    packing_hbm, token_hbm, gain_hbm, series_hbm, recon_hbm, doc_hbm, wq_ref, wk_ref, wv_ref,
    k1_ref, vt_ref, qout_ref, total_ref, norm_ref,
    packing_ref, token_ref, gain_ref, series_ref, recon_ref, doc_ref, all_ref, norms, kv_ref, q_ref, count_ref, flags, wq, wk, wv, w_sem, counts, kv_send, kv_recv, q_send, q_recv, c_send, c_recv, self_sem,
    x_send, near_recv, half_recv, pair_recv, t_send, t_recv,
):
    s = lax.axis_index("group")
    c = lax.axis_index("ctx")
    z, y = c // N_Y, lax.rem(c, N_Y)
    partner = s + 1 - 2 * lax.rem(s, 2)
    right, left, across = lax.rem(s + 2, N_GROUP), lax.rem(s + 6, N_GROUP), lax.rem(s + 4, N_GROUP)
    owner = z == s
    loads = [
        pltpu.make_async_copy(src, dst, w_sem.at[n])
        for n, (src, dst) in enumerate((
            (wk_ref, wk), (wv_ref, wv), (wq_ref, wq),
            (series_hbm, series_ref), (recon_hbm, recon_ref), (doc_hbm, doc_ref),
            (packing_hbm, packing_ref), (token_hbm, token_ref), (gain_hbm, gain_ref),
        ))
    ]
    for n in (3, 4, 5, 6, 7, 8, 0, 1, 2):
        loads[n].start()
    bar = pltpu.get_barrier_semaphore()

    def greet(o, carry):
        pl.semaphore_signal(bar, inc=1, device_id=(s, lax.rem(c + o, N_CTX)), device_id_type=MESH)
        return carry

    lax.fori_loop(1, N_CTX, greet, 0)
    for o in range(1, N_GROUP):
        pl.semaphore_signal(bar, inc=1, device_id=(lax.rem(s + o, N_GROUP), c), device_id_type=MESH)
    vt_ref[:, :, 0:16, :] = jnp.ones((PER, N_Z, 16, ROWS), jnp.bfloat16)
    norms[...] = jnp.zeros_like(norms)
    for n in range(3, 9):
        loads[n].wait()
    count_ref[...] = document_counts(doc_ref)
    normed = normed_rows(packing_ref, series_ref, recon_ref, token_ref, gain_ref, flags)

    def project(n, w):
        loads[n].wait()
        return jnp.dot(normed, w[...], preferred_element_type=jnp.float32)

    pack_keys(kv_ref, project(0, wk), project(1, wv))
    pl.semaphore_wait(bar, N_CTX - 1 + N_GROUP - 1)

    def rows_of(d):
        return pl.ds(pl.multiple_of(d * BLK, BLK), BLK)

    def send_kv(d, i):
        return pltpu.make_async_remote_copy(
            src_ref=kv_ref.at[d], dst_ref=all_ref.at[:, s, rows_of(c), :],
            send_sem=kv_send, recv_sem=kv_recv.at[i],
            device_id=(s, d), device_id_type=MESH,
        )

    def send_q(d):
        return pltpu.make_async_remote_copy(
            src_ref=q_ref.at[d], dst_ref=qout_ref.at[c], send_sem=q_send, recv_sem=q_recv,
            device_id=(s, d), device_id_type=MESH,
        )

    def send_count(t):
        return pltpu.make_async_remote_copy(
            src_ref=count_ref, dst_ref=counts.at[c], send_sem=c_send.at[t], recv_sem=c_recv,
            device_id=(s, s * N_Y + t), device_id_type=MESH,
        )

    def send_total(o):
        return pltpu.make_async_remote_copy(
            src_ref=total_ref, dst_ref=total_ref, send_sem=t_send.at[o - 1], recv_sem=t_recv,
            device_id=(lax.rem(s + o, N_GROUP), c), device_id_type=MESH,
        )

    def other(i, yy):
        return lax.rem(z + step_z(i), N_Z) * N_Y + lax.rem(y + yy, N_Y)

    own_kv = pltpu.make_async_copy(kv_ref.at[c], all_ref.at[:, s, rows_of(c), :], self_sem.at[0])
    own_q = pltpu.make_async_copy(q_ref.at[c], qout_ref.at[c], self_sem.at[1])
    own_kv.start()
    for t in range(N_Y):
        @pl.when(s * N_Y + t != c)
        def _():
            send_count(t).start()

    for yy in range(1, N_Y):
        send_kv(other(0, yy), 0).start()

    def start_plane(i, carry):
        for yy in range(N_Y):
            send_kv(other(i, yy), i).start()
        return carry

    lax.fori_loop(1, N_Z, start_plane, 0)
    pack_queries(q_ref, project(2, wq) * SCALE)
    own_q.start()

    def start_q(i, carry):
        for yy in range(N_Y):
            send_q(other(i, yy)).start()
        return carry


    def plane(i):
        return lax.rem(z + N_Z - step_z(i), N_Z)

    def hop(slot, i, to, kind, recv, half=None):
        first, size = plane(i) * 128, 128
        if half is not None:
            first, size = first + half * 64, 64
        part = all_ref.at[:, slot, pl.ds(pl.multiple_of(first, 64), size), :]
        return pltpu.make_async_remote_copy(
            src_ref=part, dst_ref=part, send_sem=x_send.at[kind], recv_sem=recv,
            device_id=(to, c), device_id_type=MESH,
        )

    def whole(slot, kind, recv, half=None):
        part = all_ref.at[:, slot, pl.ds(0, ROWS if half is None else ROWS // 2), :]
        return pltpu.make_async_remote_copy(
            src_ref=part, dst_ref=part, send_sem=x_send.at[kind], recv_sem=recv,
            device_id=(partner, c), device_id_type=MESH,
        )

    def send_own(i):
        hop(s, i, right, 0, near_recv.at[0, i]).start()
        hop(s, i, left, 1, near_recv.at[1, i]).start()
        hop(s, i, partner, 2, pair_recv.at[0, i]).start()

    def send_near(i):
        hop(left, i, left, 0, near_recv.at[0, i]).wait_recv()
        hop(left, i, right, 3, half_recv.at[0, i], half=0).start()
        hop(left, i, partner, 5, pair_recv.at[1, i]).start()
        hop(right, i, right, 1, near_recv.at[1, i]).wait_recv()
        hop(right, i, left, 4, half_recv.at[1, i], half=1).start()
        hop(right, i, partner, 6, pair_recv.at[2, i]).start()

    def send_across(i):
        hop(across, i, left, 3, half_recv.at[0, i], half=0).wait_recv()
        hop(across, i, right, 4, half_recv.at[1, i], half=1).wait_recv()
        hop(across, i, partner, 7, pair_recv.at[3, i]).start()

    slots = (partner, lax.rem(partner + 6, N_GROUP), lax.rem(partner + 2, N_GROUP), lax.rem(partner + 4, N_GROUP))
    r = lax.broadcasted_iota(jnp.int32, (128, 128), 0)
    base = ((r // BLK) * 256 + r % BLK).astype(jnp.float32)
    lane = lax.broadcasted_iota(jnp.int32, (1, 128), 1)
    low = low_half((128, 128))

    def lay_out(i):
        for n, slot in enumerate(slots):
            hop(slot, i, partner, 2, pair_recv.at[n, i]).wait_recv()
        at = plane(i)
        rows = pl.ds(pl.multiple_of(at * 128, 128), 128)
        totals = total_ref[...].astype(jnp.float32)
        lo = pltpu.roll(totals, HD + 1, 1)[0:1]
        hi = jnp.where(lane == HD + DOCS - 1, float(N_CTX * 256), pltpu.roll(totals, HD, 1)[0:1])
        first = (at * 1024).astype(jnp.float32)
        lo, hi = lo - first, hi - first
        for n in range(N_GROUP):
            own = (base >= lo - n * BLK) & (base < hi - n * BLK)
            mark = jnp.where(own, 1.0, 0.0).astype(jnp.bfloat16)
            for h in range(PER):
                k1_ref[h, n, rows, :] = jnp.where(low, all_ref[h, n, rows, :], mark)
        for h in range(PER):
            block = all_ref[h, :, rows, :].reshape(ROWS, 128).T
            vt_ref[h, at, 16:80, :] = block[HD:128]
            keys = block[0:HD].astype(jnp.float32)
            norms[h] = jnp.maximum(norms[h], jnp.sum(keys * keys, axis=0, keepdims=True))

    def arrive_plane(i):
        part = all_ref.at[:, s, pl.ds(pl.multiple_of(plane(i) * 128, 128), 128), :]
        pltpu.make_async_remote_copy(
            src_ref=part, dst_ref=part, send_sem=kv_send, recv_sem=kv_recv.at[i],
            device_id=(partner, c), device_id_type=MESH,
        ).wait_recv()

    own_kv.wait()
    three = all_ref.at[:, s, pl.ds(pl.multiple_of(z * 128, 128), 96), :]
    pltpu.make_async_remote_copy(
        src_ref=three, dst_ref=three, send_sem=kv_send, recv_sem=kv_recv.at[0],
        device_id=(partner, c), device_id_type=MESH,
    ).wait_recv()
    send_own(0)
    arrive_plane(1)
    send_own(1)
    send_near(0)
    for yy in range(1, N_Y):
        send_q(other(0, yy)).start()
    lax.fori_loop(1, N_Z, start_q, 0)
    arrive_plane(2)
    send_own(2)
    send_near(1)
    send_across(0)

    def step(i, carry):
        arrive_plane(i)
        send_own(i)
        send_near(i - 1)
        send_across(i - 2)
        lay_out(i - 3)
        return carry

    @pl.when(owner)
    def _():
        counts[c] = count_ref[...]
        rest = counts.at[pl.ds(0, N_CTX - 1)]
        pltpu.make_async_remote_copy(
            src_ref=rest, dst_ref=rest, send_sem=c_send.at[0], recv_sem=c_recv,
            device_id=(partner, c), device_id_type=MESH,
        ).wait_recv()
        total_ref[...] = jnp.sum(counts[...], axis=0)
        for o in range(1, N_GROUP):
            send_total(o).start()

    @pl.when(jnp.logical_not(owner))
    def _():
        send_total(1).wait_recv()

    lax.fori_loop(3, N_Z, step, 0)
    send_near(N_Z - 1)
    send_across(N_Z - 2)
    lay_out(N_Z - 3)
    send_across(N_Z - 1)
    lay_out(N_Z - 2)
    lay_out(N_Z - 1)
    sub = lax.broadcasted_iota(jnp.int32, (8, 128), 0)
    top = jnp.zeros((8, 128), jnp.float32)
    for h in range(PER):
        top = jnp.where(sub == h, jnp.max(norms[h], axis=1, keepdims=True), top)
    norm_ref[...] = top

    for t in range(N_Y):
        @pl.when(s * N_Y + t != c)
        def _():
            send_count(t).wait_send()

    @pl.when(owner)
    def _():
        for o in range(1, N_GROUP):
            send_total(o).wait_send()

    own_q.wait()
    rest = pltpu.make_async_remote_copy(
        src_ref=q_ref.at[pl.ds(0, N_CTX - 1)], dst_ref=qout_ref.at[pl.ds(0, N_CTX - 1)],
        send_sem=q_send, recv_sem=q_recv, device_id=(partner, c), device_id_type=MESH,
    )
    rest.wait_recv()
    rest.wait_send()
    sent = kv_ref.at[pl.ds(0, N_CTX - 1)]
    pltpu.make_async_remote_copy(
        src_ref=sent, dst_ref=sent, send_sem=kv_send, recv_sem=kv_recv.at[0],
        device_id=(partner, c), device_id_type=MESH,
    ).wait_send()
    for kind, slot in enumerate((s, s, s, left, right, left, right, across)):
        whole(slot, kind, t_recv, half=0 if kind in (3, 4) else None).wait_send()


def hbm(x):
    return pltpu.with_memory_space_constraint(x, pltpu.HBM)


def spread(packing, series, recon, token, docs, gain, w_query, w_key, w_value):
    anywhere = pl.BlockSpec(memory_space=pltpu.HBM)
    vmem = pl.BlockSpec(memory_space=pltpu.VMEM)
    dma = pltpu.SemaphoreType.DMA
    weight = pltpu.VMEM((D, D), jnp.bfloat16)
    return pl.pallas_call(
        spread_kernel,
        out_shape=(
            jax.ShapeDtypeStruct((PER, N_GROUP, ROWS, 128), jnp.bfloat16),
            jax.ShapeDtypeStruct((PER, N_Z, 80, ROWS), jnp.bfloat16),
            jax.ShapeDtypeStruct((N_CTX, QROWS, 128), jnp.bfloat16),
            jax.ShapeDtypeStruct((8, 128), jnp.int32),
            jax.ShapeDtypeStruct((8, 128), jnp.float32),
        ),
        in_specs=[anywhere] * 9,
        out_specs=(vmem, vmem, anywhere, vmem, vmem),
        scratch_shapes=[
            pltpu.SMEM((N_GROUP,), jnp.int32),
            pltpu.VMEM((D,), jnp.bfloat16),
            pltpu.VMEM((D,), jnp.bfloat16),
            pltpu.VMEM((N_GROUP, BLK, D), jnp.bfloat16),
            pltpu.VMEM((1, N_GROUP * BLK), jnp.int32),
            pltpu.VMEM((1, N_GROUP * BLK), jnp.int32),
            pltpu.VMEM((PER, N_GROUP, ROWS, 128), jnp.bfloat16),
            pltpu.VMEM((PER, 1, ROWS), jnp.float32),
            pltpu.VMEM((N_CTX, PER, BLK, 128), jnp.bfloat16),
            pltpu.VMEM((N_CTX, QROWS, 128), jnp.bfloat16),
            pltpu.VMEM((8, 128), jnp.int32),
            pltpu.VMEM((N_GROUP, BLK, 128), jnp.float32),
            weight, weight, weight,
            dma((9,)),
            pltpu.VMEM((N_CTX, 8, 128), jnp.int32),
            dma(()), dma((N_Z,)), dma(()), dma(()), dma((N_Y,)), dma(()), dma((2,)),
            dma((8,)), dma((2, N_Z)), dma((2, N_Z)), dma((4, N_Z)), dma((N_GROUP - 1,)), dma(()),
        ],
        compiler_params=pltpu.CompilerParams(
            collective_id=0, has_side_effects=True, vmem_limit_bytes=32 << 20
        ),
        name="spread",
    )(*(hbm(x) for x in (packing, token, gain, series, recon, docs, w_query, w_key, w_value)))


def attend_kernel(total_ref, norm_ref, q_ref, k1, vt, out_ref, qt, acc, top):
    s = lax.axis_index("group")
    starts = [total_ref[0, d] for d in range(3)]
    first, last = [jnp.int32(0)] + starts, starts + [jnp.int32(N_CTX * 256)]

    def edges(index):
        lo, hi = jnp.full(index.shape, N_CTX * 256), jnp.zeros(index.shape, jnp.int32)
        for d in range(DOCS):
            lo = jnp.where(index == HD + d, first[d], lo)
            hi = jnp.where(index == HD + d, last[d], hi)
        return lo, hi

    col = lax.broadcasted_iota(jnp.int32, (1, ROWS), 1)
    pos = (col // BLK) * 256 + s * BLK + col % BLK
    row = lax.broadcasted_iota(jnp.int32, (HD, 1), 0) + HD
    lo, hi = edges(row)
    own = (pos >= lo) & (pos < hi)
    far = jnp.where(own | (row >= HD + DOCS), 0.0, NEGATIVE)

    a = q_ref[:, 0:BLK, :].reshape(ROWS, 128).astype(jnp.float32).T
    b = q_ref[:, BLK:QROWS, :].astype(jnp.float32)
    b = jnp.concatenate([b, swap(b.reshape(ROWS // 2, 128)).reshape(N_CTX, 16, 128)], axis=1)
    b = b.reshape(ROWS, 128).T
    q_top = []
    for h, part in enumerate((a[0:HD], a[HD:128], b[0:HD])):
        q_top.append(jnp.max(jnp.sum(part * part, axis=0, keepdims=True)))
        qt[h] = jnp.concatenate([part, far], axis=0).astype(jnp.bfloat16)

    keys_n = KC * 256
    small = None
    for h in range(PER):
        fits = q_top[h] * norm_ref[h, 0] * 1.05 <= BOUND * BOUND
        small = fits if small is None else small & fits

    span = TQ // BLK * 256
    blocks = TQ // BLK

    def tile(t, carry):
        p0 = t * span
        p1 = p0 + span - 1
        lo, hi = jnp.int32(0), jnp.int32(N_CTX * 256)
        for st in starts:
            lo = jnp.maximum(lo, jnp.where(st <= p0, st, 0))
            hi = jnp.minimum(hi, jnp.where(st > p1, st, N_CTX * 256))
        begin, end = lo // keys_n, (hi + keys_n - 1) // keys_n
        cols = pl.ds(pl.multiple_of(t * TQ, TQ), TQ)

        def scores(h, kb):
            rows = pl.ds(pl.multiple_of(kb * KC * BLK, KC * BLK), KC * BLK)
            keys = k1[h, :, rows, :].reshape(keys_n, 128)
            return jnp.dot(keys, qt[h, :, cols], preferred_element_type=jnp.float32)

        def summed(h, kb, p):
            return jnp.dot(vt[h, kb], p, preferred_element_type=jnp.float32)

        acc[...] = jnp.zeros_like(acc)

        @pl.when(small)
        def _():
            def body(kb, carry):
                weights = [scores(h, kb) for h in range(PER)]
                weights = [jnp.exp2(w).astype(jnp.bfloat16) for w in weights]
                sums = [summed(h, kb, weights[h]) for h in range(PER)]
                for h in range(PER):
                    acc[h] += sums[h]
                return carry

            lax.fori_loop(begin, end, body, 0)

        @pl.when(jnp.logical_not(small))
        def _():
            top[...] = jnp.full_like(top, NEGATIVE)

            def body(kb, carry):
                all_scores = [scores(h, kb) for h in range(PER)]
                for h, sc in enumerate(all_scores):
                    old = top[h]
                    new = jnp.maximum(old, jnp.max(sc, axis=0, keepdims=True))
                    top[h] = new
                    weights = jnp.exp2(sc - new).astype(jnp.bfloat16)
                    acc[h] = acc[h] * jnp.exp2(old - new) + summed(h, kb, weights)
                return carry

            lax.fori_loop(begin, end, body, 0)

        def attended(h):
            return acc[h, 16:80, :] / acc[h, 0:1, :]

        here = pl.ds(t * blocks, blocks)
        o = jnp.concatenate([attended(0), attended(1)], axis=0).T
        out_ref[here, 0:BLK] = o.astype(jnp.bfloat16).reshape(blocks, BLK, 128)
        o = attended(2)
        o = jnp.concatenate([o, o], axis=0).T.reshape(blocks, BLK, 128)
        one, two = o[:, 0:16].reshape(TQ // 2, 128), o[:, 16:32].reshape(TQ // 2, 128)
        out_ref[here, BLK:QROWS] = join(one, two).astype(jnp.bfloat16).reshape(blocks, 16, 128)
        return carry

    lax.fori_loop(0, ROWS // TQ, tile, 0)


def attend(total, norms, q, k1, vt):
    vmem = pl.BlockSpec(memory_space=pltpu.VMEM)
    smem = pl.BlockSpec(memory_space=pltpu.SMEM)
    return pl.pallas_call(
        attend_kernel,
        out_shape=jax.ShapeDtypeStruct((N_CTX, QROWS, 128), jnp.bfloat16),
        in_specs=[smem, smem, vmem, vmem, vmem],
        out_specs=vmem,
        scratch_shapes=[
            pltpu.VMEM((PER, 128, ROWS), jnp.bfloat16),
            pltpu.VMEM((PER, 80, TQ), jnp.float32),
            pltpu.VMEM((PER, 1, TQ), jnp.float32),
        ],
        compiler_params=pltpu.CompilerParams(vmem_limit_bytes=32 << 20),
        name="attend",
    )(total, norms, q, k1, vt)


def finish_kernel(
    packing_ref, att_ref, series_ref, recon_ref, token_ref, w_ref, out_ref,
    got, lhs, w2, self_sem, send_sem, recv_sem,
):
    s = lax.axis_index("group")
    c = lax.axis_index("ctx")
    z, y = c // N_Y, lax.rem(c, N_Y)
    bar = pltpu.get_barrier_semaphore()

    def greet(o, carry):
        pl.semaphore_signal(bar, inc=1, device_id=(s, lax.rem(c + o, N_CTX)), device_id_type=MESH)
        return carry

    lax.fori_loop(1, N_CTX, greet, 0)
    own = pltpu.make_async_copy(att_ref.at[c], got.at[c], self_sem)
    own.start()

    def send(i, yy):
        d = lax.rem(z + step_z(i), N_Z) * N_Y + lax.rem(y + yy, N_Y)
        pltpu.make_async_remote_copy(
            src_ref=att_ref.at[d], dst_ref=got.at[c], send_sem=send_sem, recv_sem=recv_sem,
            device_id=(s, d), device_id_type=MESH,
        ).start()

    def send_plane(i, carry):
        for yy in range(N_Y):
            send(i, yy)
        return carry

    pl.semaphore_wait(bar, N_CTX - 1)
    lax.fori_loop(1, N_Z, send_plane, 0)
    for yy in range(1, N_Y):
        send(0, yy)
    order = [PER * t + n for t in range(TRIPLES) for n in range(2)] + [2, 5, 8, 11]
    for n, head in enumerate(order):
        w2[n * HD : (n + 1) * HD, :] = w_ref[head * HD : (head + 1) * HD, :]
    residual = masked_rows(series_ref[...], row_mask(recon_ref), token_ref)
    own.wait()
    rest = pltpu.make_async_remote_copy(
        src_ref=att_ref.at[pl.ds(0, N_CTX - 1)], dst_ref=got.at[pl.ds(0, N_CTX - 1)],
        send_sem=send_sem, recv_sem=recv_sem, device_id=(s, lax.rem(c + 1, N_CTX)), device_id_type=MESH,
    )
    rest.wait_recv()
    rest.wait_send()
    for k in range(N_GROUP):
        g = packing_ref[k]
        parts = [got[g * TRIPLES + t] for t in range(TRIPLES)]
        rows = slice(k * BLK, (k + 1) * BLK)
        for t in range(TRIPLES):
            lhs[rows, t * 128 : (t + 1) * 128] = parts[t][0:BLK]
        for n in range(2):
            a = parts[2 * n][BLK:QROWS].astype(jnp.float32)
            b = parts[2 * n + 1][BLK:QROWS].astype(jnp.float32)
            cols = slice((TRIPLES + n) * 128, (TRIPLES + n + 1) * 128)
            lhs[k * BLK : k * BLK + 16, cols] = join(a, swap(b)).astype(jnp.bfloat16)
            lhs[k * BLK + 16 : (k + 1) * BLK, cols] = join(swap(a), b).astype(jnp.bfloat16)
    mixed = jnp.dot(lhs[...], w2[...], preferred_element_type=jnp.float32)
    out_ref[...] = (residual + mixed).astype(jnp.bfloat16)


def finish(packing, att, series, recon, token, w_out):
    vmem = pl.BlockSpec(memory_space=pltpu.VMEM)
    return pl.pallas_call(
        finish_kernel,
        out_shape=jax.ShapeDtypeStruct(series.shape, jnp.bfloat16),
        in_specs=[pl.BlockSpec(memory_space=pltpu.SMEM)] + [vmem] * 5,
        out_specs=vmem,
        scratch_shapes=[
            pltpu.VMEM((N_CTX, QROWS, 128), jnp.bfloat16),
            pltpu.VMEM((N_GROUP * BLK, D), jnp.bfloat16),
            pltpu.VMEM((D, D), jnp.bfloat16),
            pltpu.SemaphoreType.DMA,
            pltpu.SemaphoreType.DMA,
            pltpu.SemaphoreType.DMA,
        ],
        compiler_params=pltpu.CompilerParams(
            collective_id=1, has_side_effects=True, vmem_limit_bytes=48 << 20
        ),
        name="finish",
    )(packing, att, series, recon, token, w_out)


def on_device(
    series, recon_mask, mask_token, packing_list, doc_ids, norm_gain, w_query, w_key, w_value, w_out
):
    recon = recon_mask.reshape(1, -1)
    token = mask_token
    k1, vt, q_rows, total, norms = spread(
        packing_list, series.reshape(N_GROUP, BLK, D), recon, token, doc_ids, norm_gain,
        w_query, w_key, w_value,
    )
    att = attend(total, norms, q_rows, k1, vt)
    return finish(packing_list, att, series, recon, token, w_out)


def solution(mesh):
    split = P(("group", "ctx"))
    in_specs = (
        P(("group", "ctx"), None), split, P(), split, P("group", "ctx"), P(), P(), P(), P(), P(),
    )
    return jax.shard_map(
        on_device, mesh=mesh, in_specs=in_specs, out_specs=P(("group", "ctx"), None), check_vma=False
    )
```

```python
import functools
import math

import jax
import jax.numpy as jnp
from jax import lax
from jax.experimental import pallas as pl
from jax.experimental.pallas import tpu as pltpu
from jax.sharding import PartitionSpec as P

D = 768
HEADS = 12
HD = 64
BLK = 32
N_GROUP = 8
N_CTX = 32
N_Z = 8
N_Y = 4
TRIPLES = 4
PER = 3
QROWS = 48
ROWS = N_CTX * BLK
NEGATIVE = -1e30
DOCS = 4
BOUND = 100.0
SCALE = math.log2(math.e) / math.sqrt(HD)
TQ = 256
KC = 4
MESH = pl.DeviceIdType.MESH


def low_half(shape):
    return lax.broadcasted_iota(jnp.int32, shape, len(shape) - 1) < HD


def swap(x):
    return pltpu.roll(x, HD, 1)


def join(a, b):
    return jnp.where(low_half(a.shape), a, b)


def row_mask(recon_ref):
    flags = recon_ref[...].astype(jnp.float32)
    return jnp.broadcast_to(flags, (128, flags.shape[1])).T


def masked_rows(rows, flags, token_ref):
    flags = jnp.concatenate([flags] * (D // 128), axis=1)
    token = token_ref[...].astype(jnp.float32).reshape(1, D)
    return jnp.where(flags == 1.0, token, rows.astype(jnp.float32))


def normed_rows(packing_ref, series_ref, recon_ref, token_ref, gain_ref, flags):
    flags[...] = row_mask(recon_ref).reshape(N_GROUP, BLK, 128)
    pieces = []
    for g in range(N_GROUP):
        at = jnp.int32(0)
        for k in range(1, N_GROUP):
            at = jnp.where(packing_ref[k] == g, k, at)
        pieces.append(masked_rows(series_ref[at], flags[at], token_ref))
    x = jnp.concatenate(pieces, axis=0)
    factor = lax.rsqrt(jnp.mean(x * x, axis=-1, keepdims=True) + 1e-06)
    return (x * factor * gain_ref[...].astype(jnp.float32).reshape(1, D)).astype(jnp.bfloat16)


def document_counts(doc_ref):
    ids = doc_ref[...]
    lane = lax.broadcasted_iota(jnp.int32, (8, 128), 1)
    count = jnp.zeros((8, 128), jnp.int32)
    for d in range(DOCS - 1):
        below = jnp.sum((ids <= d).astype(jnp.float32), axis=1, keepdims=True).astype(jnp.int32)
        count = jnp.where(lane == d, below, count)
    return count


def piece(values, g):
    return values[g * BLK : (g + 1) * BLK]


def pack_keys(kv_ref, key, value):
    for m in range(HEADS // 2):
        kp, vp = key[:, m * 128 : (m + 1) * 128], value[:, m * 128 : (m + 1) * 128]
        for head, kv in ((2 * m, join(kp, swap(vp))), (2 * m + 1, join(swap(kp), vp))):
            kv = kv.astype(jnp.bfloat16)
            for g in range(N_GROUP):
                kv_ref[g * TRIPLES + head // PER, head % PER] = piece(kv, g)


def pack_queries(q_ref, query):
    for t in range(TRIPLES):
        pair = [query[:, m * 128 : (m + 1) * 128] for m in (3 * t // 2, 3 * t // 2 + 1)]
        if t % 2 == 0:
            first, last = pair[0], pair[1]
        else:
            first, last = join(swap(pair[0]), swap(pair[1])), swap(pair[1])
        first = first.astype(jnp.bfloat16)
        swapped = swap(last)
        for g in range(N_GROUP):
            to = g * TRIPLES + t
            q_ref[to, 0:BLK] = piece(first, g)
            half = join(last[g * BLK : g * BLK + 16], swapped[g * BLK + 16 : (g + 1) * BLK])
            q_ref[to, BLK:QROWS] = half.astype(jnp.bfloat16)


def step_z(i):
    return lax.rem(N_Z + (1 - 2 * lax.rem(i + 1, 2)) * ((i + 1) // 2), N_Z)


def spread_kernel(
    packing_hbm, token_hbm, gain_hbm, series_hbm, recon_hbm, doc_hbm, wq_ref, wk_ref, wv_ref,
    k1_ref, vt_ref, qout_ref, total_ref, norm_ref,
    packing_ref, token_ref, gain_ref, series_ref, recon_ref, doc_ref, all_ref, norms, kv_ref, q_ref, count_ref, flags, wq, wk, wv, w_sem, counts, kv_send, kv_recv, q_send, q_recv, c_send, c_recv, self_sem,
    x_send, near_recv, half_recv, pair_recv, t_send, t_recv,
):
    s = lax.axis_index("group")
    c = lax.axis_index("ctx")
    z, y = c // N_Y, lax.rem(c, N_Y)
    partner = s + 1 - 2 * lax.rem(s, 2)
    right, left, across = lax.rem(s + 2, N_GROUP), lax.rem(s + 6, N_GROUP), lax.rem(s + 4, N_GROUP)
    owner = z == s
    loads = [
        pltpu.make_async_copy(src, dst, w_sem.at[n])
        for n, (src, dst) in enumerate((
            (wk_ref, wk), (wv_ref, wv), (wq_ref, wq),
            (series_hbm, series_ref), (recon_hbm, recon_ref), (doc_hbm, doc_ref),
            (packing_hbm, packing_ref), (token_hbm, token_ref), (gain_hbm, gain_ref),
        ))
    ]
    for n in (3, 4, 5, 6, 7, 8, 0, 1, 2):
        loads[n].start()
    bar = pltpu.get_barrier_semaphore()

    def greet(o, carry):
        pl.semaphore_signal(bar, inc=1, device_id=(s, lax.rem(c + o, N_CTX)), device_id_type=MESH)
        return carry

    lax.fori_loop(1, N_CTX, greet, 0)
    for o in range(1, N_GROUP):
        pl.semaphore_signal(bar, inc=1, device_id=(lax.rem(s + o, N_GROUP), c), device_id_type=MESH)
    vt_ref[:, :, 0:16, :] = jnp.ones((PER, N_Z, 16, ROWS), jnp.bfloat16)
    norms[...] = jnp.zeros_like(norms)
    for n in range(3, 9):
        loads[n].wait()
    count_ref[...] = document_counts(doc_ref)
    normed = normed_rows(packing_ref, series_ref, recon_ref, token_ref, gain_ref, flags)

    def project(n, w):
        loads[n].wait()
        return jnp.dot(normed, w[...], preferred_element_type=jnp.float32)

    pack_keys(kv_ref, project(0, wk), project(1, wv))
    pl.semaphore_wait(bar, N_CTX - 1 + N_GROUP - 1)

    def rows_of(d):
        return pl.ds(pl.multiple_of(d * BLK, BLK), BLK)

    def send_kv(d, i):
        return pltpu.make_async_remote_copy(
            src_ref=kv_ref.at[d], dst_ref=all_ref.at[:, s, rows_of(c), :],
            send_sem=kv_send, recv_sem=kv_recv.at[i],
            device_id=(s, d), device_id_type=MESH,
        )

    def send_q(d):
        return pltpu.make_async_remote_copy(
            src_ref=q_ref.at[d], dst_ref=qout_ref.at[c], send_sem=q_send, recv_sem=q_recv,
            device_id=(s, d), device_id_type=MESH,
        )

    def send_count(t):
        return pltpu.make_async_remote_copy(
            src_ref=count_ref, dst_ref=counts.at[c], send_sem=c_send.at[t], recv_sem=c_recv,
            device_id=(s, s * N_Y + t), device_id_type=MESH,
        )

    def send_total(o):
        return pltpu.make_async_remote_copy(
            src_ref=total_ref, dst_ref=total_ref, send_sem=t_send.at[o - 1], recv_sem=t_recv,
            device_id=(lax.rem(s + o, N_GROUP), c), device_id_type=MESH,
        )

    def other(i, yy):
        return lax.rem(z + step_z(i), N_Z) * N_Y + lax.rem(y + yy, N_Y)

    own_kv = pltpu.make_async_copy(kv_ref.at[c], all_ref.at[:, s, rows_of(c), :], self_sem.at[0])
    own_q = pltpu.make_async_copy(q_ref.at[c], qout_ref.at[c], self_sem.at[1])
    own_kv.start()
    for t in range(N_Y):
        @pl.when(s * N_Y + t != c)
        def _():
            send_count(t).start()

    for yy in range(1, N_Y):
        send_kv(other(0, yy), 0).start()

    def start_plane(i, carry):
        for yy in range(N_Y):
            send_kv(other(i, yy), i).start()
        return carry

    lax.fori_loop(1, 5, start_plane, 0)
    pack_queries(q_ref, project(2, wq) * SCALE)
    own_q.start()

    def start_q(i, carry):
        for yy in range(N_Y):
            send_q(other(i, yy)).start()
        return carry


    def plane(i):
        return lax.rem(z + N_Z - step_z(i), N_Z)

    def hop(slot, i, to, kind, recv, half=None):
        first, size = plane(i) * 128, 128
        if half is not None:
            first, size = first + half * 64, 64
        part = all_ref.at[:, slot, pl.ds(pl.multiple_of(first, 64), size), :]
        return pltpu.make_async_remote_copy(
            src_ref=part, dst_ref=part, send_sem=x_send.at[kind], recv_sem=recv,
            device_id=(to, c), device_id_type=MESH,
        )

    def whole(slot, kind, recv, half=None):
        part = all_ref.at[:, slot, pl.ds(0, ROWS if half is None else ROWS // 2), :]
        return pltpu.make_async_remote_copy(
            src_ref=part, dst_ref=part, send_sem=x_send.at[kind], recv_sem=recv,
            device_id=(partner, c), device_id_type=MESH,
        )

    def send_own(i):
        hop(s, i, right, 0, near_recv.at[0, i]).start()
        hop(s, i, left, 1, near_recv.at[1, i]).start()
        hop(s, i, partner, 2, pair_recv.at[0, i]).start()

    def send_near(i):
        hop(left, i, left, 0, near_recv.at[0, i]).wait_recv()
        hop(left, i, right, 3, half_recv.at[0, i], half=0).start()
        hop(left, i, partner, 5, pair_recv.at[1, i]).start()
        hop(right, i, right, 1, near_recv.at[1, i]).wait_recv()
        hop(right, i, left, 4, half_recv.at[1, i], half=1).start()
        hop(right, i, partner, 6, pair_recv.at[2, i]).start()

    def send_across(i):
        hop(across, i, left, 3, half_recv.at[0, i], half=0).wait_recv()
        hop(across, i, right, 4, half_recv.at[1, i], half=1).wait_recv()
        hop(across, i, partner, 7, pair_recv.at[3, i]).start()

    slots = (partner, lax.rem(partner + 6, N_GROUP), lax.rem(partner + 2, N_GROUP), lax.rem(partner + 4, N_GROUP))
    r = lax.broadcasted_iota(jnp.int32, (128, 128), 0)
    base = ((r // BLK) * 256 + r % BLK).astype(jnp.float32)
    lane = lax.broadcasted_iota(jnp.int32, (1, 128), 1)
    low = low_half((128, 128))

    def lay_out(i):
        for n, slot in enumerate(slots):
            hop(slot, i, partner, 2, pair_recv.at[n, i]).wait_recv()
        at = plane(i)
        rows = pl.ds(pl.multiple_of(at * 128, 128), 128)
        totals = total_ref[...].astype(jnp.float32)
        lo = pltpu.roll(totals, HD + 1, 1)[0:1]
        hi = jnp.where(lane == HD + DOCS - 1, float(N_CTX * 256), pltpu.roll(totals, HD, 1)[0:1])
        first = (at * 1024).astype(jnp.float32)
        lo, hi = lo - first, hi - first
        for n in range(N_GROUP):
            own = (base >= lo - n * BLK) & (base < hi - n * BLK)
            mark = jnp.where(own, 1.0, 0.0).astype(jnp.bfloat16)
            for h in range(PER):
                k1_ref[h, n, rows, :] = jnp.where(low, all_ref[h, n, rows, :], mark)
        for h in range(PER):
            block = all_ref[h, :, rows, :].reshape(ROWS, 128).T
            vt_ref[h, at, 16:80, :] = block[HD:128]
            keys = block[0:HD].astype(jnp.float32)
            norms[h] = jnp.maximum(norms[h], jnp.sum(keys * keys, axis=0, keepdims=True))

    def arrive_plane(i):
        part = all_ref.at[:, s, pl.ds(pl.multiple_of(plane(i) * 128, 128), 128), :]
        pltpu.make_async_remote_copy(
            src_ref=part, dst_ref=part, send_sem=kv_send, recv_sem=kv_recv.at[i],
            device_id=(partner, c), device_id_type=MESH,
        ).wait_recv()

    own_kv.wait()
    three = all_ref.at[:, s, pl.ds(pl.multiple_of(z * 128, 128), 96), :]
    pltpu.make_async_remote_copy(
        src_ref=three, dst_ref=three, send_sem=kv_send, recv_sem=kv_recv.at[0],
        device_id=(partner, c), device_id_type=MESH,
    ).wait_recv()
    send_own(0)
    lax.fori_loop(5, N_Z, start_plane, 0)
    arrive_plane(1)
    send_own(1)
    send_near(0)
    for yy in range(1, N_Y):
        send_q(other(0, yy)).start()
    lax.fori_loop(1, N_Z, start_q, 0)
    arrive_plane(2)
    send_own(2)
    send_near(1)
    send_across(0)

    def step(i, carry):
        arrive_plane(i)
        send_own(i)
        send_near(i - 1)
        send_across(i - 2)
        lay_out(i - 3)
        return carry

    @pl.when(owner)
    def _():
        counts[c] = count_ref[...]
        rest = counts.at[pl.ds(0, N_CTX - 1)]
        pltpu.make_async_remote_copy(
            src_ref=rest, dst_ref=rest, send_sem=c_send.at[0], recv_sem=c_recv,
            device_id=(partner, c), device_id_type=MESH,
        ).wait_recv()
        total_ref[...] = jnp.sum(counts[...], axis=0)
        for o in range(1, N_GROUP):
            send_total(o).start()

    arrive_plane(3)
    send_own(3)
    send_near(2)
    send_across(1)

    @pl.when(jnp.logical_not(owner))
    def _():
        send_total(1).wait_recv()

    lay_out(0)
    lax.fori_loop(4, N_Z, step, 0)
    send_near(N_Z - 1)
    send_across(N_Z - 2)
    lay_out(N_Z - 3)
    send_across(N_Z - 1)
    lay_out(N_Z - 2)
    lay_out(N_Z - 1)
    sub = lax.broadcasted_iota(jnp.int32, (8, 128), 0)
    top = jnp.zeros((8, 128), jnp.float32)
    for h in range(PER):
        top = jnp.where(sub == h, jnp.max(norms[h], axis=1, keepdims=True), top)
    norm_ref[...] = top

    for t in range(N_Y):
        @pl.when(s * N_Y + t != c)
        def _():
            send_count(t).wait_send()

    @pl.when(owner)
    def _():
        for o in range(1, N_GROUP):
            send_total(o).wait_send()

    own_q.wait()
    rest = pltpu.make_async_remote_copy(
        src_ref=q_ref.at[pl.ds(0, N_CTX - 1)], dst_ref=qout_ref.at[pl.ds(0, N_CTX - 1)],
        send_sem=q_send, recv_sem=q_recv, device_id=(partner, c), device_id_type=MESH,
    )
    rest.wait_recv()
    rest.wait_send()
    sent = kv_ref.at[pl.ds(0, N_CTX - 1)]
    pltpu.make_async_remote_copy(
        src_ref=sent, dst_ref=sent, send_sem=kv_send, recv_sem=kv_recv.at[0],
        device_id=(partner, c), device_id_type=MESH,
    ).wait_send()
    for kind, slot in enumerate((s, s, s, left, right, left, right, across)):
        whole(slot, kind, t_recv, half=0 if kind in (3, 4) else None).wait_send()


def hbm(x):
    return pltpu.with_memory_space_constraint(x, pltpu.HBM)


def spread(packing, series, recon, token, docs, gain, w_query, w_key, w_value):
    anywhere = pl.BlockSpec(memory_space=pltpu.HBM)
    vmem = pl.BlockSpec(memory_space=pltpu.VMEM)
    dma = pltpu.SemaphoreType.DMA
    weight = pltpu.VMEM((D, D), jnp.bfloat16)
    return pl.pallas_call(
        spread_kernel,
        out_shape=(
            jax.ShapeDtypeStruct((PER, N_GROUP, ROWS, 128), jnp.bfloat16),
            jax.ShapeDtypeStruct((PER, N_Z, 80, ROWS), jnp.bfloat16),
            jax.ShapeDtypeStruct((N_CTX, QROWS, 128), jnp.bfloat16),
            jax.ShapeDtypeStruct((8, 128), jnp.int32),
            jax.ShapeDtypeStruct((8, 128), jnp.float32),
        ),
        in_specs=[anywhere] * 9,
        out_specs=(vmem, vmem, anywhere, vmem, vmem),
        scratch_shapes=[
            pltpu.SMEM((N_GROUP,), jnp.int32),
            pltpu.VMEM((D,), jnp.bfloat16),
            pltpu.VMEM((D,), jnp.bfloat16),
            pltpu.VMEM((N_GROUP, BLK, D), jnp.bfloat16),
            pltpu.VMEM((1, N_GROUP * BLK), jnp.int32),
            pltpu.VMEM((1, N_GROUP * BLK), jnp.int32),
            pltpu.VMEM((PER, N_GROUP, ROWS, 128), jnp.bfloat16),
            pltpu.VMEM((PER, 1, ROWS), jnp.float32),
            pltpu.VMEM((N_CTX, PER, BLK, 128), jnp.bfloat16),
            pltpu.VMEM((N_CTX, QROWS, 128), jnp.bfloat16),
            pltpu.VMEM((8, 128), jnp.int32),
            pltpu.VMEM((N_GROUP, BLK, 128), jnp.float32),
            weight, weight, weight,
            dma((9,)),
            pltpu.VMEM((N_CTX, 8, 128), jnp.int32),
            dma(()), dma((N_Z,)), dma(()), dma(()), dma((N_Y,)), dma(()), dma((2,)),
            dma((8,)), dma((2, N_Z)), dma((2, N_Z)), dma((4, N_Z)), dma((N_GROUP - 1,)), dma(()),
        ],
        compiler_params=pltpu.CompilerParams(
            collective_id=0, has_side_effects=True, vmem_limit_bytes=32 << 20
        ),
        name="spread",
    )(*(hbm(x) for x in (packing, token, gain, series, recon, docs, w_query, w_key, w_value)))


def attend_kernel(total_ref, norm_ref, q_ref, k1, vt, out_ref, qt, acc, top):
    s = lax.axis_index("group")
    starts = [total_ref[0, d] for d in range(3)]
    first, last = [jnp.int32(0)] + starts, starts + [jnp.int32(N_CTX * 256)]

    def edges(index):
        lo, hi = jnp.full(index.shape, N_CTX * 256), jnp.zeros(index.shape, jnp.int32)
        for d in range(DOCS):
            lo = jnp.where(index == HD + d, first[d], lo)
            hi = jnp.where(index == HD + d, last[d], hi)
        return lo, hi

    col = lax.broadcasted_iota(jnp.int32, (1, ROWS), 1)
    pos = (col // BLK) * 256 + s * BLK + col % BLK
    row = lax.broadcasted_iota(jnp.int32, (HD, 1), 0) + HD
    lo, hi = edges(row)
    own = (pos >= lo) & (pos < hi)
    far = jnp.where(own | (row >= HD + DOCS), 0.0, NEGATIVE)

    a = q_ref[:, 0:BLK, :].reshape(ROWS, 128).astype(jnp.float32).T
    b = q_ref[:, BLK:QROWS, :].astype(jnp.float32)
    b = jnp.concatenate([b, swap(b.reshape(ROWS // 2, 128)).reshape(N_CTX, 16, 128)], axis=1)
    b = b.reshape(ROWS, 128).T
    q_top = []
    for h, part in enumerate((a[0:HD], a[HD:128], b[0:HD])):
        q_top.append(jnp.max(jnp.sum(part * part, axis=0, keepdims=True)))
        qt[h] = jnp.concatenate([part, far], axis=0).astype(jnp.bfloat16)

    keys_n = KC * 256
    small = None
    for h in range(PER):
        fits = q_top[h] * norm_ref[h, 0] * 1.05 <= BOUND * BOUND
        small = fits if small is None else small & fits

    span = TQ // BLK * 256
    blocks = TQ // BLK

    def tile(t, carry):
        p0 = t * span
        p1 = p0 + span - 1
        lo, hi = jnp.int32(0), jnp.int32(N_CTX * 256)
        for st in starts:
            lo = jnp.maximum(lo, jnp.where(st <= p0, st, 0))
            hi = jnp.minimum(hi, jnp.where(st > p1, st, N_CTX * 256))
        begin, end = lo // keys_n, (hi + keys_n - 1) // keys_n
        cols = pl.ds(pl.multiple_of(t * TQ, TQ), TQ)

        def scores(h, kb):
            rows = pl.ds(pl.multiple_of(kb * KC * BLK, KC * BLK), KC * BLK)
            keys = k1[h, :, rows, :].reshape(keys_n, 128)
            return jnp.dot(keys, qt[h, :, cols], preferred_element_type=jnp.float32)

        def summed(h, kb, p):
            return jnp.dot(vt[h, kb], p, preferred_element_type=jnp.float32)

        acc[...] = jnp.zeros_like(acc)

        @pl.when(small)
        def _():
            def body(kb, carry):
                weights = [scores(h, kb) for h in range(PER)]
                weights = [jnp.exp2(w).astype(jnp.bfloat16) for w in weights]
                sums = [summed(h, kb, weights[h]) for h in range(PER)]
                for h in range(PER):
                    acc[h] += sums[h]
                return carry

            lax.fori_loop(begin, end, body, 0)

        @pl.when(jnp.logical_not(small))
        def _():
            top[...] = jnp.full_like(top, NEGATIVE)

            def body(kb, carry):
                all_scores = [scores(h, kb) for h in range(PER)]
                for h, sc in enumerate(all_scores):
                    old = top[h]
                    new = jnp.maximum(old, jnp.max(sc, axis=0, keepdims=True))
                    top[h] = new
                    weights = jnp.exp2(sc - new).astype(jnp.bfloat16)
                    acc[h] = acc[h] * jnp.exp2(old - new) + summed(h, kb, weights)
                return carry

            lax.fori_loop(begin, end, body, 0)

        def attended(h):
            return acc[h, 16:80, :] / acc[h, 0:1, :]

        here = pl.ds(t * blocks, blocks)
        o = jnp.concatenate([attended(0), attended(1)], axis=0).T
        out_ref[here, 0:BLK] = o.astype(jnp.bfloat16).reshape(blocks, BLK, 128)
        o = attended(2)
        o = jnp.concatenate([o, o], axis=0).T.reshape(blocks, BLK, 128)
        one, two = o[:, 0:16].reshape(TQ // 2, 128), o[:, 16:32].reshape(TQ // 2, 128)
        out_ref[here, BLK:QROWS] = join(one, two).astype(jnp.bfloat16).reshape(blocks, 16, 128)
        return carry

    lax.fori_loop(0, ROWS // TQ, tile, 0)


def attend(total, norms, q, k1, vt):
    vmem = pl.BlockSpec(memory_space=pltpu.VMEM)
    smem = pl.BlockSpec(memory_space=pltpu.SMEM)
    return pl.pallas_call(
        attend_kernel,
        out_shape=jax.ShapeDtypeStruct((N_CTX, QROWS, 128), jnp.bfloat16),
        in_specs=[smem, smem, vmem, vmem, vmem],
        out_specs=vmem,
        scratch_shapes=[
            pltpu.VMEM((PER, 128, ROWS), jnp.bfloat16),
            pltpu.VMEM((PER, 80, TQ), jnp.float32),
            pltpu.VMEM((PER, 1, TQ), jnp.float32),
        ],
        compiler_params=pltpu.CompilerParams(vmem_limit_bytes=32 << 20),
        name="attend",
    )(total, norms, q, k1, vt)


def finish_kernel(
    packing_ref, att_ref, series_ref, recon_ref, token_ref, w_ref, out_ref,
    got, lhs, w2, self_sem, send_sem, recv_sem,
):
    s = lax.axis_index("group")
    c = lax.axis_index("ctx")
    z, y = c // N_Y, lax.rem(c, N_Y)
    bar = pltpu.get_barrier_semaphore()

    def greet(o, carry):
        pl.semaphore_signal(bar, inc=1, device_id=(s, lax.rem(c + o, N_CTX)), device_id_type=MESH)
        return carry

    lax.fori_loop(1, N_CTX, greet, 0)
    own = pltpu.make_async_copy(att_ref.at[c], got.at[c], self_sem)
    own.start()

    def send(i, yy):
        d = lax.rem(z + step_z(i), N_Z) * N_Y + lax.rem(y + yy, N_Y)
        pltpu.make_async_remote_copy(
            src_ref=att_ref.at[d], dst_ref=got.at[c], send_sem=send_sem, recv_sem=recv_sem,
            device_id=(s, d), device_id_type=MESH,
        ).start()

    def send_plane(i, carry):
        for yy in range(N_Y):
            send(i, yy)
        return carry

    pl.semaphore_wait(bar, N_CTX - 1)
    lax.fori_loop(1, N_Z, send_plane, 0)
    for yy in range(1, N_Y):
        send(0, yy)
    order = [PER * t + n for t in range(TRIPLES) for n in range(2)] + [2, 5, 8, 11]
    for n, head in enumerate(order):
        w2[n * HD : (n + 1) * HD, :] = w_ref[head * HD : (head + 1) * HD, :]
    residual = masked_rows(series_ref[...], row_mask(recon_ref), token_ref)
    own.wait()
    rest = pltpu.make_async_remote_copy(
        src_ref=att_ref.at[pl.ds(0, N_CTX - 1)], dst_ref=got.at[pl.ds(0, N_CTX - 1)],
        send_sem=send_sem, recv_sem=recv_sem, device_id=(s, lax.rem(c + 1, N_CTX)), device_id_type=MESH,
    )
    rest.wait_recv()
    rest.wait_send()
    for k in range(N_GROUP):
        g = packing_ref[k]
        parts = [got[g * TRIPLES + t] for t in range(TRIPLES)]
        rows = slice(k * BLK, (k + 1) * BLK)
        for t in range(TRIPLES):
            lhs[rows, t * 128 : (t + 1) * 128] = parts[t][0:BLK]
        for n in range(2):
            a = parts[2 * n][BLK:QROWS].astype(jnp.float32)
            b = parts[2 * n + 1][BLK:QROWS].astype(jnp.float32)
            cols = slice((TRIPLES + n) * 128, (TRIPLES + n + 1) * 128)
            lhs[k * BLK : k * BLK + 16, cols] = join(a, swap(b)).astype(jnp.bfloat16)
            lhs[k * BLK + 16 : (k + 1) * BLK, cols] = join(swap(a), b).astype(jnp.bfloat16)
    mixed = jnp.dot(lhs[...], w2[...], preferred_element_type=jnp.float32)
    out_ref[...] = (residual + mixed).astype(jnp.bfloat16)


def finish(packing, att, series, recon, token, w_out):
    vmem = pl.BlockSpec(memory_space=pltpu.VMEM)
    return pl.pallas_call(
        finish_kernel,
        out_shape=jax.ShapeDtypeStruct(series.shape, jnp.bfloat16),
        in_specs=[pl.BlockSpec(memory_space=pltpu.SMEM)] + [vmem] * 5,
        out_specs=vmem,
        scratch_shapes=[
            pltpu.VMEM((N_CTX, QROWS, 128), jnp.bfloat16),
            pltpu.VMEM((N_GROUP * BLK, D), jnp.bfloat16),
            pltpu.VMEM((D, D), jnp.bfloat16),
            pltpu.SemaphoreType.DMA,
            pltpu.SemaphoreType.DMA,
            pltpu.SemaphoreType.DMA,
        ],
        compiler_params=pltpu.CompilerParams(
            collective_id=1, has_side_effects=True, vmem_limit_bytes=48 << 20
        ),
        name="finish",
    )(packing, att, series, recon, token, w_out)


def on_device(
    series, recon_mask, mask_token, packing_list, doc_ids, norm_gain, w_query, w_key, w_value, w_out
):
    recon = recon_mask.reshape(1, -1)
    token = mask_token
    k1, vt, q_rows, total, norms = spread(
        packing_list, series.reshape(N_GROUP, BLK, D), recon, token, doc_ids, norm_gain,
        w_query, w_key, w_value,
    )
    att = attend(total, norms, q_rows, k1, vt)
    return finish(packing_list, att, series, recon, token, w_out)


def solution(mesh):
    split = P(("group", "ctx"))
    in_specs = (
        P(("group", "ctx"), None), split, P(), split, P("group", "ctx"), P(), P(), P(), P(), P(),
    )
    return jax.shard_map(
        on_device, mesh=mesh, in_specs=in_specs, out_specs=P(("group", "ctx"), None), check_vma=False
    )
```

```python
import functools
import math

import jax
import jax.numpy as jnp
from jax import lax
from jax.experimental import pallas as pl
from jax.experimental.pallas import tpu as pltpu
from jax.sharding import PartitionSpec as P

D = 768
HEADS = 12
HD = 64
BLK = 32
N_GROUP = 8
N_CTX = 32
N_Z = 8
N_Y = 4
TRIPLES = 4
PER = 3
QROWS = 48
ROWS = N_CTX * BLK
NEGATIVE = -1e30
DOCS = 4
BOUND = 100.0
SCALE = math.log2(math.e) / math.sqrt(HD)
TQ = 256
KC = 4
MESH = pl.DeviceIdType.MESH


def low_half(shape):
    return lax.broadcasted_iota(jnp.int32, shape, len(shape) - 1) < HD


def swap(x):
    return pltpu.roll(x, HD, 1)


def join(a, b):
    return jnp.where(low_half(a.shape), a, b)


def row_mask(recon_ref):
    flags = recon_ref[...].astype(jnp.float32)
    return jnp.broadcast_to(flags, (128, flags.shape[1])).T


def masked_rows(rows, flags, token_ref):
    flags = jnp.concatenate([flags] * (D // 128), axis=1)
    token = token_ref[...].astype(jnp.float32).reshape(1, D)
    return jnp.where(flags == 1.0, token, rows.astype(jnp.float32))


def normed_rows(packing_ref, series_ref, recon_ref, token_ref, gain_ref, flags):
    flags[...] = row_mask(recon_ref).reshape(N_GROUP, BLK, 128)
    pieces = []
    for g in range(N_GROUP):
        at = jnp.int32(0)
        for k in range(1, N_GROUP):
            at = jnp.where(packing_ref[k] == g, k, at)
        pieces.append(masked_rows(series_ref[at], flags[at], token_ref))
    x = jnp.concatenate(pieces, axis=0)
    factor = lax.rsqrt(jnp.mean(x * x, axis=-1, keepdims=True) + 1e-06)
    return (x * factor * gain_ref[...].astype(jnp.float32).reshape(1, D)).astype(jnp.bfloat16)


def document_counts(doc_ref):
    ids = doc_ref[...]
    lane = lax.broadcasted_iota(jnp.int32, (8, 128), 1)
    count = jnp.zeros((8, 128), jnp.int32)
    for d in range(DOCS - 1):
        below = jnp.sum((ids <= d).astype(jnp.float32), axis=1, keepdims=True).astype(jnp.int32)
        count = jnp.where(lane == d, below, count)
    return count


def piece(values, g):
    return values[g * BLK : (g + 1) * BLK]


def pack_keys(kv_ref, key, value):
    for m in range(HEADS // 2):
        kp, vp = key[:, m * 128 : (m + 1) * 128], value[:, m * 128 : (m + 1) * 128]
        for head, kv in ((2 * m, join(kp, swap(vp))), (2 * m + 1, join(swap(kp), vp))):
            kv = kv.astype(jnp.bfloat16)
            for g in range(N_GROUP):
                kv_ref[g * TRIPLES + head // PER, head % PER] = piece(kv, g)


def pack_queries(q_ref, query):
    for t in range(TRIPLES):
        pair = [query[:, m * 128 : (m + 1) * 128] for m in (3 * t // 2, 3 * t // 2 + 1)]
        if t % 2 == 0:
            first, last = pair[0], pair[1]
        else:
            first, last = join(swap(pair[0]), swap(pair[1])), swap(pair[1])
        first = first.astype(jnp.bfloat16)
        swapped = swap(last)
        for g in range(N_GROUP):
            to = g * TRIPLES + t
            q_ref[to, 0:BLK] = piece(first, g)
            half = join(last[g * BLK : g * BLK + 16], swapped[g * BLK + 16 : (g + 1) * BLK])
            q_ref[to, BLK:QROWS] = half.astype(jnp.bfloat16)


def step_z(i):
    return lax.rem(N_Z + (1 - 2 * lax.rem(i + 1, 2)) * ((i + 1) // 2), N_Z)


def spread_kernel(
    packing_hbm, token_hbm, gain_hbm, series_hbm, recon_hbm, doc_hbm, wq_ref, wk_ref, wv_ref,
    k1_ref, vt_ref, qout_ref, total_ref, norm_ref,
    packing_ref, token_ref, gain_ref, series_ref, recon_ref, doc_ref, all_ref, norms, kv_ref, q_ref, count_ref, flags, wq, wk, wv, w_sem, counts, kv_send, kv_recv, q_send, q_recv, c_send, c_recv, self_sem,
    x_send, near_recv, half_recv, pair_recv, t_send, t_recv,
):
    s = lax.axis_index("group")
    c = lax.axis_index("ctx")
    z, y = c // N_Y, lax.rem(c, N_Y)
    partner = s + 1 - 2 * lax.rem(s, 2)
    right, left, across = lax.rem(s + 2, N_GROUP), lax.rem(s + 6, N_GROUP), lax.rem(s + 4, N_GROUP)
    owner = z == s
    loads = [
        pltpu.make_async_copy(src, dst, w_sem.at[n])
        for n, (src, dst) in enumerate((
            (wk_ref, wk), (wv_ref, wv), (wq_ref, wq),
            (series_hbm, series_ref), (recon_hbm, recon_ref), (doc_hbm, doc_ref),
            (packing_hbm, packing_ref), (token_hbm, token_ref), (gain_hbm, gain_ref),
        ))
    ]
    for n in (3, 4, 5, 6, 7, 8, 0, 1, 2):
        loads[n].start()
    bar = pltpu.get_barrier_semaphore()

    def greet(o, carry):
        pl.semaphore_signal(bar, inc=1, device_id=(s, lax.rem(c + o, N_CTX)), device_id_type=MESH)
        return carry

    lax.fori_loop(1, N_CTX, greet, 0)
    for o in range(1, N_GROUP):
        pl.semaphore_signal(bar, inc=1, device_id=(lax.rem(s + o, N_GROUP), c), device_id_type=MESH)
    vt_ref[:, :, 0:16, :] = jnp.ones((PER, N_Z, 16, ROWS), jnp.bfloat16)
    norms[...] = jnp.zeros_like(norms)
    for n in range(3, 9):
        loads[n].wait()
    count_ref[...] = document_counts(doc_ref)
    normed = normed_rows(packing_ref, series_ref, recon_ref, token_ref, gain_ref, flags)

    def project(n, w):
        loads[n].wait()
        return jnp.dot(normed, w[...], preferred_element_type=jnp.float32)

    pack_keys(kv_ref, project(0, wk), project(1, wv))
    pl.semaphore_wait(bar, N_CTX - 1 + N_GROUP - 1)

    def rows_of(d):
        return pl.ds(pl.multiple_of(d * BLK, BLK), BLK)

    def send_kv(d, i):
        return pltpu.make_async_remote_copy(
            src_ref=kv_ref.at[d], dst_ref=all_ref.at[:, s, rows_of(c), :],
            send_sem=kv_send, recv_sem=kv_recv.at[i],
            device_id=(s, d), device_id_type=MESH,
        )

    def send_q(d):
        return pltpu.make_async_remote_copy(
            src_ref=q_ref.at[d], dst_ref=qout_ref.at[c], send_sem=q_send, recv_sem=q_recv,
            device_id=(s, d), device_id_type=MESH,
        )

    def send_count(t):
        return pltpu.make_async_remote_copy(
            src_ref=count_ref, dst_ref=counts.at[c], send_sem=c_send.at[t], recv_sem=c_recv,
            device_id=(s, s * N_Y + t), device_id_type=MESH,
        )

    def send_total(o):
        return pltpu.make_async_remote_copy(
            src_ref=total_ref, dst_ref=total_ref, send_sem=t_send.at[o - 1], recv_sem=t_recv,
            device_id=(lax.rem(s + o, N_GROUP), c), device_id_type=MESH,
        )

    def other(i, yy):
        return lax.rem(z + step_z(i), N_Z) * N_Y + lax.rem(y + yy, N_Y)

    own_kv = pltpu.make_async_copy(kv_ref.at[c], all_ref.at[:, s, rows_of(c), :], self_sem.at[0])
    own_q = pltpu.make_async_copy(q_ref.at[c], qout_ref.at[c], self_sem.at[1])
    own_kv.start()
    for t in range(N_Y):
        @pl.when(s * N_Y + t != c)
        def _():
            send_count(t).start()

    for yy in range(1, N_Y):
        send_kv(other(0, yy), 0).start()

    def start_plane(i, carry):
        for yy in range(N_Y):
            send_kv(other(i, yy), i).start()
        return carry

    lax.fori_loop(1, 3, start_plane, 0)
    pack_queries(q_ref, project(2, wq) * SCALE)
    own_q.start()

    def start_q(i, carry):
        for yy in range(N_Y):
            send_q(other(i, yy)).start()
        return carry


    def plane(i):
        return lax.rem(z + N_Z - step_z(i), N_Z)

    def hop(slot, i, to, kind, recv, half=None):
        first, size = plane(i) * 128, 128
        if half is not None:
            first, size = first + half * 64, 64
        part = all_ref.at[:, slot, pl.ds(pl.multiple_of(first, 64), size), :]
        return pltpu.make_async_remote_copy(
            src_ref=part, dst_ref=part, send_sem=x_send.at[kind], recv_sem=recv,
            device_id=(to, c), device_id_type=MESH,
        )

    def whole(slot, kind, recv, half=None):
        part = all_ref.at[:, slot, pl.ds(0, ROWS if half is None else ROWS // 2), :]
        return pltpu.make_async_remote_copy(
            src_ref=part, dst_ref=part, send_sem=x_send.at[kind], recv_sem=recv,
            device_id=(partner, c), device_id_type=MESH,
        )

    def send_own(i):
        hop(s, i, right, 0, near_recv.at[0, i]).start()
        hop(s, i, left, 1, near_recv.at[1, i]).start()
        hop(s, i, partner, 2, pair_recv.at[0, i]).start()

    def send_near(i):
        hop(left, i, left, 0, near_recv.at[0, i]).wait_recv()
        hop(left, i, right, 3, half_recv.at[0, i], half=0).start()
        hop(left, i, partner, 5, pair_recv.at[1, i]).start()
        hop(right, i, right, 1, near_recv.at[1, i]).wait_recv()
        hop(right, i, left, 4, half_recv.at[1, i], half=1).start()
        hop(right, i, partner, 6, pair_recv.at[2, i]).start()

    def send_across(i):
        hop(across, i, left, 3, half_recv.at[0, i], half=0).wait_recv()
        hop(across, i, right, 4, half_recv.at[1, i], half=1).wait_recv()
        hop(across, i, partner, 7, pair_recv.at[3, i]).start()

    slots = (partner, lax.rem(partner + 6, N_GROUP), lax.rem(partner + 2, N_GROUP), lax.rem(partner + 4, N_GROUP))
    r = lax.broadcasted_iota(jnp.int32, (128, 128), 0)
    base = ((r // BLK) * 256 + r % BLK).astype(jnp.float32)
    lane = lax.broadcasted_iota(jnp.int32, (1, 128), 1)
    low = low_half((128, 128))

    def lay_out(i):
        for n, slot in enumerate(slots):
            hop(slot, i, partner, 2, pair_recv.at[n, i]).wait_recv()
        at = plane(i)
        rows = pl.ds(pl.multiple_of(at * 128, 128), 128)
        totals = total_ref[...].astype(jnp.float32)
        lo = pltpu.roll(totals, HD + 1, 1)[0:1]
        hi = jnp.where(lane == HD + DOCS - 1, float(N_CTX * 256), pltpu.roll(totals, HD, 1)[0:1])
        first = (at * 1024).astype(jnp.float32)
        lo, hi = lo - first, hi - first
        for n in range(N_GROUP):
            own = (base >= lo - n * BLK) & (base < hi - n * BLK)
            mark = jnp.where(own, 1.0, 0.0).astype(jnp.bfloat16)
            for h in range(PER):
                k1_ref[h, n, rows, :] = jnp.where(low, all_ref[h, n, rows, :], mark)
        for h in range(PER):
            block = all_ref[h, :, rows, :].reshape(ROWS, 128).T
            vt_ref[h, at, 16:80, :] = block[HD:128]
            keys = block[0:HD].astype(jnp.float32)
            norms[h] = jnp.maximum(norms[h], jnp.sum(keys * keys, axis=0, keepdims=True))

    def arrive_plane(i):
        part = all_ref.at[:, s, pl.ds(pl.multiple_of(plane(i) * 128, 128), 128), :]
        pltpu.make_async_remote_copy(
            src_ref=part, dst_ref=part, send_sem=kv_send, recv_sem=kv_recv.at[i],
            device_id=(partner, c), device_id_type=MESH,
        ).wait_recv()

    own_kv.wait()
    three = all_ref.at[:, s, pl.ds(pl.multiple_of(z * 128, 128), 96), :]
    pltpu.make_async_remote_copy(
        src_ref=three, dst_ref=three, send_sem=kv_send, recv_sem=kv_recv.at[0],
        device_id=(partner, c), device_id_type=MESH,
    ).wait_recv()
    send_own(0)
    lax.fori_loop(3, 6, start_plane, 0)
    arrive_plane(1)
    send_own(1)
    lax.fori_loop(6, N_Z, start_plane, 0)
    send_near(0)
    for yy in range(1, N_Y):
        send_q(other(0, yy)).start()
    lax.fori_loop(1, N_Z, start_q, 0)
    arrive_plane(2)
    send_own(2)
    send_near(1)
    send_across(0)

    def step(i, carry):
        arrive_plane(i)
        send_own(i)
        send_near(i - 1)
        send_across(i - 2)
        lay_out(i - 3)
        return carry

    @pl.when(owner)
    def _():
        counts[c] = count_ref[...]
        rest = counts.at[pl.ds(0, N_CTX - 1)]
        pltpu.make_async_remote_copy(
            src_ref=rest, dst_ref=rest, send_sem=c_send.at[0], recv_sem=c_recv,
            device_id=(partner, c), device_id_type=MESH,
        ).wait_recv()
        total_ref[...] = jnp.sum(counts[...], axis=0)
        for o in range(1, N_GROUP):
            send_total(o).start()

    arrive_plane(3)
    send_own(3)
    send_near(2)
    send_across(1)

    @pl.when(jnp.logical_not(owner))
    def _():
        send_total(1).wait_recv()

    lay_out(0)
    lax.fori_loop(4, N_Z, step, 0)
    send_near(N_Z - 1)
    send_across(N_Z - 2)
    lay_out(N_Z - 3)
    send_across(N_Z - 1)
    lay_out(N_Z - 2)
    lay_out(N_Z - 1)
    sub = lax.broadcasted_iota(jnp.int32, (8, 128), 0)
    top = jnp.zeros((8, 128), jnp.float32)
    for h in range(PER):
        top = jnp.where(sub == h, jnp.max(norms[h], axis=1, keepdims=True), top)
    norm_ref[...] = top

    for t in range(N_Y):
        @pl.when(s * N_Y + t != c)
        def _():
            send_count(t).wait_send()

    @pl.when(owner)
    def _():
        for o in range(1, N_GROUP):
            send_total(o).wait_send()

    own_q.wait()
    rest = pltpu.make_async_remote_copy(
        src_ref=q_ref.at[pl.ds(0, N_CTX - 1)], dst_ref=qout_ref.at[pl.ds(0, N_CTX - 1)],
        send_sem=q_send, recv_sem=q_recv, device_id=(partner, c), device_id_type=MESH,
    )
    rest.wait_recv()
    rest.wait_send()
    sent = kv_ref.at[pl.ds(0, N_CTX - 1)]
    pltpu.make_async_remote_copy(
        src_ref=sent, dst_ref=sent, send_sem=kv_send, recv_sem=kv_recv.at[0],
        device_id=(partner, c), device_id_type=MESH,
    ).wait_send()
    for kind, slot in enumerate((s, s, s, left, right, left, right, across)):
        whole(slot, kind, t_recv, half=0 if kind in (3, 4) else None).wait_send()


def hbm(x):
    return pltpu.with_memory_space_constraint(x, pltpu.HBM)


def spread(packing, series, recon, token, docs, gain, w_query, w_key, w_value):
    anywhere = pl.BlockSpec(memory_space=pltpu.HBM)
    vmem = pl.BlockSpec(memory_space=pltpu.VMEM)
    dma = pltpu.SemaphoreType.DMA
    weight = pltpu.VMEM((D, D), jnp.bfloat16)
    return pl.pallas_call(
        spread_kernel,
        out_shape=(
            jax.ShapeDtypeStruct((PER, N_GROUP, ROWS, 128), jnp.bfloat16),
            jax.ShapeDtypeStruct((PER, N_Z, 80, ROWS), jnp.bfloat16),
            jax.ShapeDtypeStruct((N_CTX, QROWS, 128), jnp.bfloat16),
            jax.ShapeDtypeStruct((8, 128), jnp.int32),
            jax.ShapeDtypeStruct((8, 128), jnp.float32),
        ),
        in_specs=[anywhere] * 9,
        out_specs=(vmem, vmem, anywhere, vmem, vmem),
        scratch_shapes=[
            pltpu.SMEM((N_GROUP,), jnp.int32),
            pltpu.VMEM((D,), jnp.bfloat16),
            pltpu.VMEM((D,), jnp.bfloat16),
            pltpu.VMEM((N_GROUP, BLK, D), jnp.bfloat16),
            pltpu.VMEM((1, N_GROUP * BLK), jnp.int32),
            pltpu.VMEM((1, N_GROUP * BLK), jnp.int32),
            pltpu.VMEM((PER, N_GROUP, ROWS, 128), jnp.bfloat16),
            pltpu.VMEM((PER, 1, ROWS), jnp.float32),
            pltpu.VMEM((N_CTX, PER, BLK, 128), jnp.bfloat16),
            pltpu.VMEM((N_CTX, QROWS, 128), jnp.bfloat16),
            pltpu.VMEM((8, 128), jnp.int32),
            pltpu.VMEM((N_GROUP, BLK, 128), jnp.float32),
            weight, weight, weight,
            dma((9,)),
            pltpu.VMEM((N_CTX, 8, 128), jnp.int32),
            dma(()), dma((N_Z,)), dma(()), dma(()), dma((N_Y,)), dma(()), dma((2,)),
            dma((8,)), dma((2, N_Z)), dma((2, N_Z)), dma((4, N_Z)), dma((N_GROUP - 1,)), dma(()),
        ],
        compiler_params=pltpu.CompilerParams(
            collective_id=0, has_side_effects=True, vmem_limit_bytes=32 << 20
        ),
        name="spread",
    )(*(hbm(x) for x in (packing, token, gain, series, recon, docs, w_query, w_key, w_value)))


def attend_kernel(total_ref, norm_ref, q_ref, k1, vt, out_ref, qt, acc, top):
    s = lax.axis_index("group")
    starts = [total_ref[0, d] for d in range(3)]
    first, last = [jnp.int32(0)] + starts, starts + [jnp.int32(N_CTX * 256)]

    def edges(index):
        lo, hi = jnp.full(index.shape, N_CTX * 256), jnp.zeros(index.shape, jnp.int32)
        for d in range(DOCS):
            lo = jnp.where(index == HD + d, first[d], lo)
            hi = jnp.where(index == HD + d, last[d], hi)
        return lo, hi

    col = lax.broadcasted_iota(jnp.int32, (1, ROWS), 1)
    pos = (col // BLK) * 256 + s * BLK + col % BLK
    row = lax.broadcasted_iota(jnp.int32, (HD, 1), 0) + HD
    lo, hi = edges(row)
    own = (pos >= lo) & (pos < hi)
    far = jnp.where(own | (row >= HD + DOCS), 0.0, NEGATIVE)

    a = q_ref[:, 0:BLK, :].reshape(ROWS, 128).astype(jnp.float32).T
    b = q_ref[:, BLK:QROWS, :].astype(jnp.float32)
    b = jnp.concatenate([b, swap(b.reshape(ROWS // 2, 128)).reshape(N_CTX, 16, 128)], axis=1)
    b = b.reshape(ROWS, 128).T
    q_top = []
    for h, part in enumerate((a[0:HD], a[HD:128], b[0:HD])):
        q_top.append(jnp.max(jnp.sum(part * part, axis=0, keepdims=True)))
        qt[h] = jnp.concatenate([part, far], axis=0).astype(jnp.bfloat16)

    keys_n = KC * 256
    small = None
    for h in range(PER):
        fits = q_top[h] * norm_ref[h, 0] * 1.05 <= BOUND * BOUND
        small = fits if small is None else small & fits

    span = TQ // BLK * 256
    blocks = TQ // BLK

    def tile(t, carry):
        p0 = t * span
        p1 = p0 + span - 1
        lo, hi = jnp.int32(0), jnp.int32(N_CTX * 256)
        for st in starts:
            lo = jnp.maximum(lo, jnp.where(st <= p0, st, 0))
            hi = jnp.minimum(hi, jnp.where(st > p1, st, N_CTX * 256))
        begin, end = lo // keys_n, (hi + keys_n - 1) // keys_n
        cols = pl.ds(pl.multiple_of(t * TQ, TQ), TQ)

        def scores(h, kb):
            rows = pl.ds(pl.multiple_of(kb * KC * BLK, KC * BLK), KC * BLK)
            keys = k1[h, :, rows, :].reshape(keys_n, 128)
            return jnp.dot(keys, qt[h, :, cols], preferred_element_type=jnp.float32)

        def summed(h, kb, p):
            return jnp.dot(vt[h, kb], p, preferred_element_type=jnp.float32)

        acc[...] = jnp.zeros_like(acc)

        @pl.when(small)
        def _():
            def body(kb, carry):
                weights = [scores(h, kb) for h in range(PER)]
                weights = [jnp.exp2(w).astype(jnp.bfloat16) for w in weights]
                sums = [summed(h, kb, weights[h]) for h in range(PER)]
                for h in range(PER):
                    acc[h] += sums[h]
                return carry

            lax.fori_loop(begin, end, body, 0)

        @pl.when(jnp.logical_not(small))
        def _():
            top[...] = jnp.full_like(top, NEGATIVE)

            def body(kb, carry):
                all_scores = [scores(h, kb) for h in range(PER)]
                for h, sc in enumerate(all_scores):
                    old = top[h]
                    new = jnp.maximum(old, jnp.max(sc, axis=0, keepdims=True))
                    top[h] = new
                    weights = jnp.exp2(sc - new).astype(jnp.bfloat16)
                    acc[h] = acc[h] * jnp.exp2(old - new) + summed(h, kb, weights)
                return carry

            lax.fori_loop(begin, end, body, 0)

        def attended(h):
            return acc[h, 16:80, :] / acc[h, 0:1, :]

        here = pl.ds(t * blocks, blocks)
        o = jnp.concatenate([attended(0), attended(1)], axis=0).T
        out_ref[here, 0:BLK] = o.astype(jnp.bfloat16).reshape(blocks, BLK, 128)
        o = attended(2)
        o = jnp.concatenate([o, o], axis=0).T.reshape(blocks, BLK, 128)
        one, two = o[:, 0:16].reshape(TQ // 2, 128), o[:, 16:32].reshape(TQ // 2, 128)
        out_ref[here, BLK:QROWS] = join(one, two).astype(jnp.bfloat16).reshape(blocks, 16, 128)
        return carry

    lax.fori_loop(0, ROWS // TQ, tile, 0)


def attend(total, norms, q, k1, vt):
    vmem = pl.BlockSpec(memory_space=pltpu.VMEM)
    smem = pl.BlockSpec(memory_space=pltpu.SMEM)
    return pl.pallas_call(
        attend_kernel,
        out_shape=jax.ShapeDtypeStruct((N_CTX, QROWS, 128), jnp.bfloat16),
        in_specs=[smem, smem, vmem, vmem, vmem],
        out_specs=vmem,
        scratch_shapes=[
            pltpu.VMEM((PER, 128, ROWS), jnp.bfloat16),
            pltpu.VMEM((PER, 80, TQ), jnp.float32),
            pltpu.VMEM((PER, 1, TQ), jnp.float32),
        ],
        compiler_params=pltpu.CompilerParams(vmem_limit_bytes=32 << 20),
        name="attend",
    )(total, norms, q, k1, vt)


def finish_kernel(
    packing_ref, att_ref, series_ref, recon_ref, token_ref, w_ref, out_ref,
    got, lhs, w2, self_sem, send_sem, recv_sem,
):
    s = lax.axis_index("group")
    c = lax.axis_index("ctx")
    z, y = c // N_Y, lax.rem(c, N_Y)
    bar = pltpu.get_barrier_semaphore()

    def greet(o, carry):
        pl.semaphore_signal(bar, inc=1, device_id=(s, lax.rem(c + o, N_CTX)), device_id_type=MESH)
        return carry

    lax.fori_loop(1, N_CTX, greet, 0)
    own = pltpu.make_async_copy(att_ref.at[c], got.at[c], self_sem)
    own.start()

    def send(i, yy):
        d = lax.rem(z + step_z(i), N_Z) * N_Y + lax.rem(y + yy, N_Y)
        pltpu.make_async_remote_copy(
            src_ref=att_ref.at[d], dst_ref=got.at[c], send_sem=send_sem, recv_sem=recv_sem,
            device_id=(s, d), device_id_type=MESH,
        ).start()

    def send_plane(i, carry):
        for yy in range(N_Y):
            send(i, yy)
        return carry

    pl.semaphore_wait(bar, N_CTX - 1)
    lax.fori_loop(1, N_Z, send_plane, 0)
    for yy in range(1, N_Y):
        send(0, yy)
    order = [PER * t + n for t in range(TRIPLES) for n in range(2)] + [2, 5, 8, 11]
    for n, head in enumerate(order):
        w2[n * HD : (n + 1) * HD, :] = w_ref[head * HD : (head + 1) * HD, :]
    residual = masked_rows(series_ref[...], row_mask(recon_ref), token_ref)
    own.wait()
    rest = pltpu.make_async_remote_copy(
        src_ref=att_ref.at[pl.ds(0, N_CTX - 1)], dst_ref=got.at[pl.ds(0, N_CTX - 1)],
        send_sem=send_sem, recv_sem=recv_sem, device_id=(s, lax.rem(c + 1, N_CTX)), device_id_type=MESH,
    )
    rest.wait_recv()
    rest.wait_send()
    for k in range(N_GROUP):
        g = packing_ref[k]
        parts = [got[g * TRIPLES + t] for t in range(TRIPLES)]
        rows = slice(k * BLK, (k + 1) * BLK)
        for t in range(TRIPLES):
            lhs[rows, t * 128 : (t + 1) * 128] = parts[t][0:BLK]
        for n in range(2):
            a = parts[2 * n][BLK:QROWS].astype(jnp.float32)
            b = parts[2 * n + 1][BLK:QROWS].astype(jnp.float32)
            cols = slice((TRIPLES + n) * 128, (TRIPLES + n + 1) * 128)
            lhs[k * BLK : k * BLK + 16, cols] = join(a, swap(b)).astype(jnp.bfloat16)
            lhs[k * BLK + 16 : (k + 1) * BLK, cols] = join(swap(a), b).astype(jnp.bfloat16)
    mixed = jnp.dot(lhs[...], w2[...], preferred_element_type=jnp.float32)
    out_ref[...] = (residual + mixed).astype(jnp.bfloat16)


def finish(packing, att, series, recon, token, w_out):
    vmem = pl.BlockSpec(memory_space=pltpu.VMEM)
    return pl.pallas_call(
        finish_kernel,
        out_shape=jax.ShapeDtypeStruct(series.shape, jnp.bfloat16),
        in_specs=[pl.BlockSpec(memory_space=pltpu.SMEM)] + [vmem] * 5,
        out_specs=vmem,
        scratch_shapes=[
            pltpu.VMEM((N_CTX, QROWS, 128), jnp.bfloat16),
            pltpu.VMEM((N_GROUP * BLK, D), jnp.bfloat16),
            pltpu.VMEM((D, D), jnp.bfloat16),
            pltpu.SemaphoreType.DMA,
            pltpu.SemaphoreType.DMA,
            pltpu.SemaphoreType.DMA,
        ],
        compiler_params=pltpu.CompilerParams(
            collective_id=1, has_side_effects=True, vmem_limit_bytes=48 << 20
        ),
        name="finish",
    )(packing, att, series, recon, token, w_out)


def on_device(
    series, recon_mask, mask_token, packing_list, doc_ids, norm_gain, w_query, w_key, w_value, w_out
):
    recon = recon_mask.reshape(1, -1)
    token = mask_token
    k1, vt, q_rows, total, norms = spread(
        packing_list, series.reshape(N_GROUP, BLK, D), recon, token, doc_ids, norm_gain,
        w_query, w_key, w_value,
    )
    att = attend(total, norms, q_rows, k1, vt)
    return finish(packing_list, att, series, recon, token, w_out)


def solution(mesh):
    split = P(("group", "ctx"))
    in_specs = (
        P(("group", "ctx"), None), split, P(), split, P("group", "ctx"), P(), P(), P(), P(), P(),
    )
    return jax.shard_map(
        on_device, mesh=mesh, in_specs=in_specs, out_specs=P(("group", "ctx"), None), check_vma=False
    )
```
